256 devices in a mesh: dp: 64 (over x, z_hi, y), section: 4 (over z_lo, core).
Axes of the slice: x: 4, y: 4, z: 8 (z_hi: 4, z_lo: 2; z = z_hi * 2 + z_lo), core: 2. Of those that a mesh axis runs over, the one named last changes fastest.
Arguments:
- inputs: bfloat16 [2, 4096, 1024], P(None, 'dp'), may hold values from -6 to 6
- ln_gain: float32 [4, 1024], P('section'), may hold values from 0.5 to 1.5
- w_in: bfloat16 [4, 1024, 2048], P('section'), may hold values from -0.1875 to 0.1875
- w_out: bfloat16 [4, 2048, 1024], P('section'), may hold values from -0.125 to 0.125
- layer_scale: float32 [4, 1024], P('section'), may hold values from 0.25 to 1
- out_grad: bfloat16 [2, 4096, 1024], P(None, 'dp'), may hold values from -6 to 6
- owner_table: int32 [64], replicated, may hold values from 0 to 63, each once
Outputs:
- act_factor: float32 [4, 1024, 1024], P('section', 'dp')
- grad_factor: float32 [4, 2048, 2048], P('section', 'dp')
The draws below stay inside these ranges and needn't reach their ends.
Inputs may be any that keep to these rules, and one draw needn't show every extreme that they name: owner_table holds each of 0 .. 63 once.
All inputs are finite; a program needn't handle non-finite values.
Results may differ from the reference program's by a relative error of at most 0.009.
Values may be sent and summed in bfloat16 or wider, within the bound.
A program may use at most 128 MiB of HBM per device.

```python
import math
import jax
import jax.numpy as jnp
from jax import lax

C = 1024
H = 2048
MB = 2
SECTIONS = 4
TOKENS = 4096
N_DP = 64


def block_scale(stream_key, shape, cuts, low, high):
    gain, own = 1.0, jax.random.fold_in(stream_key, 6)
    for position, shards_of in cuts:
        steps = jnp.exp(jax.random.uniform(jax.random.fold_in(own, position), (shards_of,), jnp.float32, low / len(cuts), high / len(cuts)))
        gain = gain * jnp.repeat(steps, shape[position] // shards_of).reshape([-1 if axis == position else 1 for axis in range(len(shape))])
    return gain


def centred(stream_key, extent, scale, most, cuts=(), dtype=jnp.bfloat16):
    array = scale * jax.random.normal(stream_key, extent, jnp.float32)
    if cuts:
        array = array * block_scale(stream_key, extent, cuts, -0.22, 0.18)
    return jnp.clip(array, -most, most).astype(dtype)


def setup_inputs(seed: int = 0) -> dict:
    keys = jax.random.split(jax.random.key(seed), 8)
    inputs = centred(keys[0], (MB, TOKENS, C), 1.0, 6.0, ((1, 64),))
    ln_gain = jnp.clip(1.0 + 0.1 * jax.random.normal(keys[1], (SECTIONS, C), jnp.float32), 0.5, 1.5)
    w_in = centred(keys[2], (SECTIONS, C, H), C ** -0.5, 0.1875, ((0, 4),))
    w_out = centred(keys[3], (SECTIONS, H, C), H ** -0.5, 0.125, ((0, 4),))
    layer_scale = jnp.clip(jnp.exp(math.log(1.0) - 1.3862944 * jax.random.uniform(keys[4], (SECTIONS, C), jnp.float32) ** block_scale(keys[4], (SECTIONS, C), ((0, 4),), -0.2, 0.2)), 0.25, 1.0)
    out_grad = centred(keys[5], (MB, TOKENS, C), 1.0, 6.0, ((1, 64),))
    owner_table = jax.random.permutation(keys[6], N_DP).astype(jnp.int32)
    return {"inputs": inputs, "ln_gain": ln_gain, "w_in": w_in, "w_out": w_out, "layer_scale": layer_scale, "out_grad": out_grad, "owner_table": owner_table}


SQRT_HALF = 0.7071067811865476
INV_ROOT_TAU = 0.3989422804014327

def gelu_exact(values):
    return 0.5 * values * (1.0 + jax.scipy.special.erf(values * SQRT_HALF))

def gelu_slope(values):
    return 0.5 * (1.0 + jax.scipy.special.erf(values * SQRT_HALF)) + values * INV_ROOT_TAU * jnp.exp(-0.5 * values * values)

def normalize(activations, gain_row):
    floats = activations.astype(jnp.float32)
    center = floats - lax.optimization_barrier(jnp.mean(floats, axis=-1, keepdims=True))
    inv_std = lax.rsqrt(lax.optimization_barrier(jnp.mean(center * center, axis=-1, keepdims=True)) + 1e-06)
    normed = center * inv_std
    return ((normed * gain_row).astype(jnp.bfloat16), normed, inv_std)

def forward_block(activations, gain_row, weight_in, weight_out, scales):
    normed_bf, normed, inv_std = normalize(activations, gain_row)
    hidden = jnp.dot(normed_bf, weight_in, preferred_element_type=jnp.float32)
    activated = gelu_exact(hidden).astype(jnp.bfloat16)
    branch = jnp.dot(activated, weight_out, preferred_element_type=jnp.float32)
    output = (activations.astype(jnp.float32) + scales * branch).astype(jnp.bfloat16)
    return (output, normed_bf, normed, inv_std, hidden)

def backward_block(cotangent, normed, inv_std, hidden, gain_row, weight_in, weight_out, scales):
    scaled = (cotangent.astype(jnp.float32) * scales).astype(jnp.bfloat16)
    grad_act = lax.dot_general(scaled, weight_out, (((1,), (1,)), ((), ())), preferred_element_type=jnp.float32)
    grad_hidden = (grad_act * gelu_slope(hidden)).astype(jnp.bfloat16)
    grad_normed = lax.dot_general(grad_hidden, weight_in, (((1,), (1,)), ((), ())), preferred_element_type=jnp.float32) * gain_row
    mean_one = lax.optimization_barrier(jnp.mean(grad_normed, axis=-1, keepdims=True))
    mean_two = lax.optimization_barrier(jnp.mean(grad_normed * normed, axis=-1, keepdims=True))
    grad_input = cotangent.astype(jnp.float32) + inv_std * (grad_normed - mean_one - normed * mean_two)
    return (grad_input.astype(jnp.bfloat16), grad_hidden)

def reorder(square, owner_table):
    owners = owner_table.shape[0]
    blocks = square.reshape(owners, square.shape[0] // owners, square.shape[1])
    return jnp.take(blocks, owner_table, axis=0).reshape(square.shape)

def reference(inputs, ln_gain, w_in, w_out, layer_scale, out_grad, owner_table):
    section_count = ln_gain.shape[0]
    batch_count = inputs.shape[0]
    kept_bf = [[] for section_step in range(section_count)]
    kept_normed = [[] for section_step in range(section_count)]
    kept_inv = [[] for section_step in range(section_count)]
    kept_hidden = [[] for section_step in range(section_count)]
    kept_grads = [[] for section_step in range(section_count)]
    for batch_step in range(batch_count):
        activations = inputs[batch_step]
        for section_step in range(section_count):
            activations, normed_bf, normed, inv_std, hidden = forward_block(activations, ln_gain[section_step], w_in[section_step], w_out[section_step], layer_scale[section_step])
            kept_bf[section_step].append(normed_bf)
            kept_normed[section_step].append(normed)
            kept_inv[section_step].append(inv_std)
            kept_hidden[section_step].append(hidden)
    for batch_step in range(batch_count):
        cotangent = out_grad[batch_step]
        for section_step in reversed(range(section_count)):
            cotangent, grad_hidden = backward_block(cotangent, kept_normed[section_step][batch_step], kept_inv[section_step][batch_step], kept_hidden[section_step][batch_step], ln_gain[section_step], w_in[section_step], w_out[section_step], layer_scale[section_step])
            kept_grads[section_step].append(grad_hidden)
    total_rows = batch_count * inputs.shape[1]
    act_list = []
    grad_list = []
    for section_step in range(section_count):
        act_rows = jnp.concatenate(kept_bf[section_step], axis=0)
        grad_rows = jnp.concatenate(kept_grads[section_step], axis=0)
        act_square = jnp.dot(act_rows.T, act_rows, preferred_element_type=jnp.float32) / total_rows
        grad_square = jnp.dot(grad_rows.T, grad_rows, preferred_element_type=jnp.float32) / total_rows
        act_list.append(reorder(act_square, owner_table))
        grad_list.append(reorder(grad_square, owner_table))
    return (jnp.stack(act_list), jnp.stack(grad_list))
```

```python
import functools
import jax
import jax.numpy as jnp
from jax import lax
from jax.experimental import pallas as pl
from jax.experimental.pallas import tpu as pltpu
from jax.sharding import PartitionSpec as P

SQRT_HALF = 0.7071067811865476
INV_ROOT_TAU = 0.3989422804014327
MESH = pl.DeviceIdType.MESH
F32 = jnp.float32
BF16 = jnp.bfloat16
NT = (((1,), (1,)), ((), ()))


def cube_side(count):
    side = 1
    while side**3 < count:
        side += 1
    return side


def kernel(
    dp_count,
    sections,
    owner_ref,
    x_ref,
    top_ref,
    gain_ref,
    scale_ref,
    win_hbm,
    wout_hbm,
    act_ref,
    grad_ref,
    win,
    wout,
    x_in,
    y_out,
    g_in,
    g_out,
    normed,
    inv_std,
    slope,
    accum,
    pick_a,
    pick_g,
    rows_a,
    rows_g,
    send_a,
    send_g,
    recv_a,
    recv_g,
    sum_a,
    sum_g,
    zsend_a,
    zsend_g,
    zrecv_a,
    zrecv_g,
    w_sem,
    relay_s,
    relay_r,
    ga_s,
    ga_r,
    gg_s,
    gg_r,
    ra_s,
    ra_r,
    rg_s,
    rg_r,
    za_s,
    za_r,
    zg_s,
    zg_r,
):
    side = cube_side(dp_count)
    sec = lax.axis_index("section")
    me = lax.axis_index("dp")
    cx = me // (side * side)
    cz = lax.rem(me // side, side)
    cy = lax.rem(me, side)
    batches, rows, width = x_ref.shape
    hidden_width = win.shape[1]
    block_a = width // dp_count
    block_g = hidden_width // dp_count
    chunk = min(256, hidden_width)
    chunks = hidden_width // chunk
    total_rows = batches * rows * dp_count

    def index_of(px, pz, py):
        return px * side * side + pz * side + py

    def x_peer(k):
        return index_of(lax.rem(cx + k, side), cz, cy)

    def y_peer(k):
        return index_of(cx, cz, lax.rem(cy + k, side))

    def z_peer(k):
        return index_of(cx, lax.rem(cz + k, side), cy)

    def remote(src, dst, ssem, rsem, device):
        return pltpu.make_async_remote_copy(
            src_ref=src, dst_ref=dst, send_sem=ssem, recv_sem=rsem,
            device_id=device, device_id_type=MESH,
        )

    steps = range(1, side)
    load_in = pltpu.make_async_copy(win_hbm, win, w_sem.at[0])
    load_out = pltpu.make_async_copy(wout_hbm, wout, w_sem.at[1])
    load_in.start()
    load_out.start()

    barrier = pltpu.get_barrier_semaphore()
    for k in steps:
        for peer in (x_peer(k), y_peer(k), z_peer(k)):
            pl.semaphore_signal(barrier, inc=1, device_id=(peer, sec), device_id_type=MESH)

    for shift in (1, sections - 1):
        pl.semaphore_signal(
            barrier, inc=1, device_id=(me, lax.rem(sec + shift, sections)), device_id_type=MESH
        )

    def barrier_wait():
        pl.semaphore_wait(barrier, 3 * (side - 1) + 2)

    def build_picks():
        for pick, block in ((pick_a, block_a), (pick_g, block_g)):
            extent = pick.shape[2]
            offset = lax.broadcasted_iota(jnp.int32, (block, extent), 1) - lax.broadcasted_iota(
                jnp.int32, (block, extent), 0
            )
            for m in range(2):
                for q in range(side):
                    for zz in range(side):
                        owner = owner_ref[index_of(cx, zz, q) if m == 0 else index_of(q, zz, cy)]
                        row = (q * side + zz) * block
                        pick[m, row : row + block, :] = jnp.where(
                            offset == owner * block, 1.0, 0.0
                        ).astype(BF16)

    forward_copies = [
        remote(y_out.at[m], x_in.at[m], relay_s.at[m], relay_r.at[m], (me, lax.rem(sec + 1, sections)))
        for m in range(batches)
    ]
    backward_copies = [
        remote(
            g_out.at[m], g_in.at[m], relay_s.at[2 + m], relay_r.at[2 + m],
            (me, lax.rem(sec + sections - 1, sections)),
        )
        for m in range(batches)
    ]
    own = (cx, cy)

    def gather_copies(buffer, ssem, rsem):
        return [
            remote(
                buffer.at[m, own[m]], buffer.at[m, own[m]], ssem.at[m, k - 1], rsem.at[m, k - 1],
                (x_peer(k) if m == 0 else y_peer(k), sec),
            )
            for m in range(2)
            for k in steps
        ]

    gather_a = gather_copies(rows_a, ga_s, ga_r)
    gather_g = gather_copies(rows_g, gg_s, gg_r)

    def scatter_copy(send, recv, ssem, rsem, m, k):
        return remote(
            send.at[m, k - 1], recv.at[m, k - 1], ssem.at[m, k - 1], rsem.at[m, k - 1],
            (y_peer(k) if m == 0 else x_peer(k), sec),
        )

    def z_copy(send, recv, ssem, rsem, k):
        return remote(send.at[k - 1], recv.at[k - 1], ssem.at[k - 1], rsem.at[k - 1], (z_peer(k), sec))

    def products(rows_ref, pick, block, send, total, recv, ssem, rsem):
        span = side * block
        extent = rows_ref.shape[3]
        for k in list(steps)[::-1] + [0]:
            for m in range(2):
                axis = cy if m == 0 else cx
                dest = lax.rem(axis + k, side)
                gathered = rows_ref[m].reshape(side * rows, extent)
                chosen = pick[m, pl.ds(pl.multiple_of(dest * span, span), span), :]
                left = lax.dot_general(chosen, gathered, NT, preferred_element_type=F32).astype(BF16)
                part = jnp.dot(left, gathered, preferred_element_type=F32)
                if k:
                    send[m, k - 1] = part.astype(BF16)
                    scatter_copy(send, recv, ssem, rsem, m, k).start()
                elif m == 0:
                    total[...] = part
                else:
                    total[...] += part

    def collect(block, send, total, recv, zsend, zrecv, ssem, rsem, zs, zr):
        for k in steps:
            for m in range(2):
                scatter_copy(send, recv, ssem, rsem, m, k).wait_recv()
        value = total[...]
        for k in steps:
            for m in range(2):
                value = value + recv[m, k - 1].astype(F32)
        total[...] = value
        for k in steps:
            dest = lax.rem(cz + k, side)
            zsend[k - 1] = total[pl.ds(pl.multiple_of(dest * block, block), block), :].astype(BF16)
            z_copy(zsend, zrecv, zs, zr, k).start()

    def finish(block, total, zsend, zrecv, zs, zr, out):
        for k in steps:
            z_copy(zsend, zrecv, zs, zr, k).wait_recv()
        value = total[pl.ds(pl.multiple_of(cz * block, block), block), :]
        for k in steps:
            value = value + zrecv[k - 1].astype(F32)
        out[...] = value / total_rows

    gain = gain_ref[...]
    scales = scale_ref[...]

    @pl.when(sec > 0)
    def _():
        build_picks()
        for copy in forward_copies:
            copy.wait_recv()

    @pl.when(sec == 0)
    def _():
        x_in[...] = x_ref[...]

    floats = x_in[...].reshape(batches * rows, width).astype(F32)
    center = floats - jnp.mean(floats, axis=-1, keepdims=True)
    inverse = lax.rsqrt(jnp.mean(center * center, axis=-1, keepdims=True) + 1e-06)
    normal = center * inverse
    normed[...] = normal
    inv_std[...] = inverse
    scaled_rows = (normal * gain).astype(BF16)
    rows_a[0, cx] = scaled_rows[:rows]
    rows_a[1, cy] = scaled_rows[rows:]
    accum[...] = jnp.zeros_like(accum)
    load_in.wait()
    load_out.wait()
    for j in range(chunks):
        cols = slice(j * chunk, (j + 1) * chunk)
        hidden = jnp.dot(scaled_rows, win[:, cols], preferred_element_type=F32)
        cdf = 0.5 * (1.0 + lax.erf(hidden * SQRT_HALF))
        activated = (hidden * cdf).astype(BF16)
        slope[:, cols] = cdf + hidden * INV_ROOT_TAU * jnp.exp(-0.5 * hidden * hidden)
        accum[...] += jnp.dot(activated, wout[cols, :], preferred_element_type=F32)

    barrier_wait()

    @pl.when(sec < sections - 1)
    def _():
        for m in range(batches):
            part = slice(m * rows, (m + 1) * rows)
            y_out[m] = (x_in[m].astype(F32) + scales * accum[part, :]).astype(BF16)
            forward_copies[m].start()

    for copy in gather_a:
        copy.start()

    @pl.when(sec == 0)
    def _():
        build_picks()

    def first_a():
        for copy in gather_a:
            copy.wait_recv()
        products(rows_a, pick_a, block_a, send_a, sum_a, recv_a, ra_s, ra_r)

    @pl.when(sec < sections - 1)
    def _():
        first_a()

    @pl.when(sec < sections - 1)
    def _():
        for copy in backward_copies:
            copy.wait_recv()

    @pl.when(sec == sections - 1)
    def _():
        g_in[...] = top_ref[...]

    cot = g_in[...].reshape(batches * rows, width).astype(F32)
    gz = (cot * scales).astype(BF16)
    accum[...] = jnp.zeros_like(accum)
    for j in range(chunks):
        cols = slice(j * chunk, (j + 1) * chunk)
        grad_act = lax.dot_general(gz, wout[cols, :], NT, preferred_element_type=F32)
        grad_hidden = (grad_act * slope[:, cols]).astype(BF16)
        rows_g[0, cx, :, cols] = grad_hidden[:rows]
        rows_g[1, cy, :, cols] = grad_hidden[rows:]

        @pl.when(sec > 0)
        def _():
            accum[...] += lax.dot_general(
                grad_hidden, win[:, cols], NT, preferred_element_type=F32
            )

    @pl.when(sec > 0)
    def _():
        for m in range(batches):
            part = slice(m * rows, (m + 1) * rows)
            normal_part = normed[part, :]
            grad_normed = accum[part, :] * gain
            mean_one = jnp.mean(grad_normed, axis=-1, keepdims=True)
            mean_two = jnp.mean(grad_normed * normal_part, axis=-1, keepdims=True)
            grad_input = g_in[m].astype(F32) + inv_std[part, :] * (
                grad_normed - mean_one - normal_part * mean_two
            )
            g_out[m] = grad_input.astype(BF16)
            backward_copies[m].start()

    for copy in gather_g:
        copy.start()

    @pl.when(sec == sections - 1)
    def _():
        first_a()

    collect(block_a, send_a, sum_a, recv_a, zsend_a, zrecv_a, ra_s, ra_r, za_s, za_r)
    for copy in gather_g:
        copy.wait_recv()
    products(rows_g, pick_g, block_g, send_g, sum_g, recv_g, rg_s, rg_r)
    finish(block_a, sum_a, zsend_a, zrecv_a, za_s, za_r, act_ref)
    collect(block_g, send_g, sum_g, recv_g, zsend_g, zrecv_g, rg_s, rg_r, zg_s, zg_r)
    finish(block_g, sum_g, zsend_g, zrecv_g, zg_s, zg_r, grad_ref)

    @pl.when(sec < sections - 1)
    def _():
        for copy in forward_copies:
            copy.wait_send()

    @pl.when(sec > 0)
    def _():
        for copy in backward_copies:
            copy.wait_send()

    for copy in gather_a + gather_g:
        copy.wait_send()
    for k in steps:
        for m in range(2):
            scatter_copy(send_a, recv_a, ra_s, ra_r, m, k).wait_send()
            scatter_copy(send_g, recv_g, rg_s, rg_r, m, k).wait_send()
        z_copy(zsend_a, zrecv_a, za_s, za_r, k).wait_send()
        z_copy(zsend_g, zrecv_g, zg_s, zg_r, k).wait_send()


def body(dp_count, sections, inputs, ln_gain, w_in, w_out, layer_scale, out_grad, owner_table):
    batches, rows, width = inputs.shape
    hidden_width = w_in.shape[2]
    side = cube_side(dp_count)
    block_a = width // dp_count
    block_g = hidden_width // dp_count
    span_a, span_g = side * block_a, side * block_g
    tokens = batches * rows
    dma = pltpu.SemaphoreType.DMA
    vmem = pl.BlockSpec(memory_space=pltpu.VMEM)
    hbm = pl.BlockSpec(memory_space=pl.ANY)
    act, grad = pl.pallas_call(
        functools.partial(kernel, dp_count, sections),
        out_shape=(
            jax.ShapeDtypeStruct((block_a, width), F32),
            jax.ShapeDtypeStruct((block_g, hidden_width), F32),
        ),
        in_specs=[pl.BlockSpec(memory_space=pltpu.SMEM), vmem, vmem, vmem, vmem, hbm, hbm],
        out_specs=(vmem, vmem),
        scratch_shapes=[
            pltpu.VMEM((width, hidden_width), BF16),
            pltpu.VMEM((hidden_width, width), BF16),
            pltpu.VMEM((batches, rows, width), BF16),
            pltpu.VMEM((batches, rows, width), BF16),
            pltpu.VMEM((batches, rows, width), BF16),
            pltpu.VMEM((batches, rows, width), BF16),
            pltpu.VMEM((tokens, width), F32),
            pltpu.VMEM((tokens, 1), F32),
            pltpu.VMEM((tokens, hidden_width), F32),
            pltpu.VMEM((tokens, width), F32),
            pltpu.VMEM((2, side * span_a, width), BF16),
            pltpu.VMEM((2, side * span_g, hidden_width), BF16),
            pltpu.VMEM((2, side, rows, width), BF16),
            pltpu.VMEM((2, side, rows, hidden_width), BF16),
            pltpu.VMEM((2, side - 1, span_a, width), BF16),
            pltpu.VMEM((2, side - 1, span_g, hidden_width), BF16),
            pltpu.VMEM((2, side - 1, span_a, width), BF16),
            pltpu.VMEM((2, side - 1, span_g, hidden_width), BF16),
            pltpu.VMEM((span_a, width), F32),
            pltpu.VMEM((span_g, hidden_width), F32),
            pltpu.VMEM((side - 1, block_a, width), BF16),
            pltpu.VMEM((side - 1, block_g, hidden_width), BF16),
            pltpu.VMEM((side - 1, block_a, width), BF16),
            pltpu.VMEM((side - 1, block_g, hidden_width), BF16),
            dma((2,)),
            dma((4,)),
            dma((4,)),
        ]
        + [dma((2, side - 1)) for _ in range(8)]
        + [dma((side - 1,)) for _ in range(4)],
        compiler_params=pltpu.CompilerParams(
            collective_id=0, has_side_effects=True, vmem_limit_bytes=60 * 1024 * 1024
        ),
        name="window",
    )(owner_table, inputs, out_grad, ln_gain, layer_scale, w_in[0], w_out[0])
    return (act[None], grad[None])


def solution(mesh):
    placed = (
        P(None, "dp", None),
        P("section", None),
        P("section", None, None),
        P("section", None, None),
        P("section", None),
        P(None, "dp", None),
        P(),
    )
    return jax.shard_map(
        functools.partial(body, mesh.shape["dp"], mesh.shape["section"]),
        mesh=mesh,
        in_specs=placed,
        out_specs=(P("section", "dp", None), P("section", "dp", None)),
        check_vma=False,
    )
```

```python
import functools
import jax
import jax.numpy as jnp
from jax import lax
from jax.experimental import pallas as pl
from jax.experimental.pallas import tpu as pltpu
from jax.sharding import PartitionSpec as P

SQRT_HALF = 0.7071067811865476
INV_ROOT_TAU = 0.3989422804014327
MESH = pl.DeviceIdType.MESH
F32 = jnp.float32
BF16 = jnp.bfloat16
NT = (((1,), (1,)), ((), ()))


RING = 4
HALVES = 2


def kernel(
    dp_count,
    sections,
    owner_ref,
    x_hbm,
    top_hbm,
    gain_ref,
    scale_ref,
    win_hbm,
    wout_hbm,
    act_ref,
    grad_ref,
    win,
    wout,
    x_in,
    y_out,
    g_in,
    g_out,
    normed,
    inv_std,
    slope,
    accum,
    *rest,
):
    (pick_a, rows_a, left_a, far_a, near_a, hold_a, sum_a, far_in_a, near_in_a, zs_a, zr_a) = rest[:11]
    (pick_g, rows_g, left_g, far_g, near_g, hold_g, sum_g, far_in_g, near_in_g, zs_g, zr_g) = rest[11:22]
    (w_sem, io_sem, relay_s, relay_r, gat_s, gat_r, sca_s, sca_r, z_s, z_r) = rest[22:]
    planes = dp_count // (RING * RING)
    sec = lax.axis_index("section")
    me = lax.axis_index("dp")
    cx = me // (planes * RING)
    cz = lax.rem(me // RING, planes)
    cy = lax.rem(me, RING)
    even = lax.rem(sec, 2) == 0
    batches, rows, width = x_in.shape
    tokens = batches * rows
    hidden_width = win.shape[1]
    block_a = width // dp_count
    block_g = hidden_width // dp_count
    chunk = min(256, hidden_width // HALVES)
    chunks = hidden_width // chunk
    total_rows = tokens * dp_count

    def index_of(px, pz, py):
        return px * planes * RING + pz * RING + py

    p = jnp.where(even, cx, cy)
    q = jnp.where(even, cy, cx)

    def at_pq(pp, pz, qq):
        return index_of(jnp.where(even, pp, qq), pz, jnp.where(even, qq, pp))

    def ring(value, k):
        return lax.rem(value + k + RING, RING)

    def p_peer(k):
        return (at_pq(ring(p, k), cz, q), sec)

    def q_peer(k):
        return (at_pq(p, cz, ring(q, k)), sec)

    def z_peer(k):
        return (index_of(cx, lax.rem(cz + k, planes), cy), sec)

    def remote(src, dst, ssem, rsem, device):
        return pltpu.make_async_remote_copy(
            src_ref=src, dst_ref=dst, send_sem=ssem, recv_sem=rsem,
            device_id=device, device_id_type=MESH,
        )

    load_in = []
    load_out = []
    for j in range(chunks):
        cols = pl.ds(j * chunk, chunk)
        load_in.append(pltpu.make_async_copy(win_hbm.at[:, cols], win.at[:, cols], w_sem.at[0, j]))
        load_out.append(pltpu.make_async_copy(wout_hbm.at[cols, :], wout.at[cols, :], w_sem.at[1, j]))
    load_x = pltpu.make_async_copy(x_hbm, x_in, io_sem.at[0])
    load_top = pltpu.make_async_copy(top_hbm, g_in, io_sem.at[1])

    @pl.when(sec == 0)
    def _():
        load_x.start()

    for j in range(chunks):
        load_in[j].start()
        load_out[j].start()

    @pl.when(sec == sections - 1)
    def _():
        load_top.start()

    barrier = pltpu.get_barrier_semaphore()
    greeted = [p_peer(1), p_peer(-1), q_peer(1), q_peer(-1)]
    greeted += [z_peer(k) for k in range(1, planes)]
    greeted += [(me, lax.rem(sec + 1, sections)), (me, lax.rem(sec + sections - 1, sections))]
    for device in greeted:
        pl.semaphore_signal(barrier, inc=1, device_id=device, device_id_type=MESH)

    def build_picks():
        for pick, block in ((pick_a, block_a), (pick_g, block_g)):
            extent = pick.shape[1]
            offset = lax.broadcasted_iota(jnp.int32, (block, extent), 1) - lax.broadcasted_iota(
                jnp.int32, (block, extent), 0
            )
            for qq in range(RING):
                for zz in range(planes):
                    owner = owner_ref[at_pq(p, zz, qq)]
                    row = (qq * planes + zz) * block
                    pick[row : row + block, :] = jnp.where(offset == owner * block, 1.0, 0.0).astype(BF16)

    forward_copies = [
        remote(y_out.at[m], x_in.at[m], relay_s.at[m], relay_r.at[m], (me, lax.rem(sec + 1, sections)))
        for m in range(batches)
    ]
    backward_copies = [
        remote(
            g_out.at[m], g_in.at[m], relay_s.at[batches + m], relay_r.at[batches + m],
            (me, lax.rem(sec + sections - 1, sections)),
        )
        for m in range(batches)
    ]

    class Factor:
        pass

    def factor(number, block, groups, pick, buffers):
        f = Factor()
        f.block, f.span, f.groups, f.pick = block, planes * block, groups, pick
        (f.rows, f.left, f.far, f.near, f.hold, f.total, f.far_in, f.near_in, f.zs, f.zr) = buffers
        f.half = f.far.shape[3]
        gs, gr = gat_s.at[number], gat_r.at[number]

        def row_copy(slot, h, n, k):
            return remote(f.rows.at[h, slot], f.rows.at[h, slot], gs.at[n], gr.at[n], p_peer(k))

        f.send_half = [[row_copy(p, h, h, 1), row_copy(p, h, 3 + h, -1)] for h in range(HALVES)]
        f.pass_on = [row_copy(ring(p, -1), 0, 2, 1), row_copy(ring(p, 1), 1, 5, -1)]
        f.gathers = [c for pair in f.send_half for c in pair] + f.pass_on
        ss, sr = sca_s.at[number], sca_r.at[number]
        f.far_copy = [
            [
                remote(f.far.at[g, d], f.far_in.at[g, d], ss.at[g, d], sr.at[g, d], q_peer((1, -1)[d]))
                for d in range(2)
            ]
            for g in range(groups)
        ]
        f.near_copy = [
            [
                [
                    remote(
                        f.near.at[g, d, h], f.near_in.at[g, d, h], ss.at[g, 2 + 2 * d + h],
                        sr.at[g, 2 + 2 * d + h], q_peer((1, -1)[d]),
                    )
                    for h in range(2)
                ]
                for d in range(2)
            ]
            for g in range(groups)
        ]
        f.z_copy = [
            [
                remote(
                    f.zs.at[g, k - 1], f.zr.at[g, k - 1], z_s.at[number, g, k - 1],
                    z_r.at[number, g, k - 1], z_peer(k),
                )
                for k in range(1, planes)
            ]
            for g in range(groups)
        ]
        return f

    fa = factor(0, block_a, 1, pick_a, (rows_a, left_a, far_a, near_a, hold_a, sum_a, far_in_a, near_in_a, zs_a, zr_a))
    fg = factor(1, block_g, 2, pick_g, (rows_g, left_g, far_g, near_g, hold_g, sum_g, far_in_g, near_in_g, zs_g, zr_g))

    def start_half(f, h):
        for copy in f.send_half[h]:
            copy.start()

    def finish_gather(f):
        f.send_half[0][0].wait_recv()
        f.pass_on[0].start()
        f.send_half[1][1].wait_recv()
        f.pass_on[1].start()
        f.send_half[0][1].wait_recv()
        f.send_half[1][0].wait_recv()
        f.pass_on[0].wait_recv()
        f.pass_on[1].wait_recv()

    def choose(f):
        extent = f.rows.shape[3]
        picked = None
        for h in range(HALVES):
            source = f.rows[h].reshape(RING * tokens, extent)
            part = lax.dot_general(
                f.pick[:, h * extent : (h + 1) * extent], source, NT, preferred_element_type=F32
            )
            picked = part if picked is None else picked + part
        f.left[...] = picked.astype(BF16)

    def part_of(f, g, k):
        extent = f.rows.shape[3]
        dest = ring(q, k)
        left = f.left[pl.ds(pl.multiple_of(dest * f.span, f.span), f.span), :]
        pieces = [
            jnp.dot(left, f.rows[h].reshape(RING * tokens, extent), preferred_element_type=F32)
            for h in ((g,) if f.groups == 2 else range(HALVES))
        ]
        return pieces[0] if len(pieces) == 1 else jnp.concatenate(pieces, axis=1)

    def far_part(f, g):
        part = part_of(f, g, 2)
        for d in range(2):
            f.far[g, d] = part[:, d * f.half : (d + 1) * f.half].astype(BF16)
            f.far_copy[g][d].start()

    def near_part(f, g, d):
        part = part_of(f, g, (1, -1)[d])
        free = 1 - d
        f.near[g, d, free] = part[:, free * f.half : (free + 1) * f.half].astype(BF16)
        f.near_copy[g][d][free].start()
        f.hold[g, d] = part[:, d * f.half : (d + 1) * f.half]

    def own_part(f, g):
        f.total[g] = part_of(f, g, 0)

    def relay_part(f, g):
        for d in range(2):
            f.far_copy[g][d].wait_recv()
            f.near[g, d, d] = (f.hold[g, d] + f.far_in[g, d].astype(F32)).astype(BF16)
            f.near_copy[g][d][d].start()

    def collect(f, g):
        for d in range(2):
            for h in range(2):
                f.near_copy[g][d][h].wait_recv()
        for h in range(2):
            cols = slice(h * f.half, (h + 1) * f.half)
            f.total[g, :, cols] += f.near_in[g, 0, h].astype(F32) + f.near_in[g, 1, h].astype(F32)
        for k in range(1, planes):
            dest = lax.rem(cz + k, planes)
            f.zs[g, k - 1] = f.total[g, pl.ds(pl.multiple_of(dest * f.block, f.block), f.block), :].astype(BF16)
            f.z_copy[g][k - 1].start()

    def finish(f, g, out):
        for copy in f.z_copy[g]:
            copy.wait_recv()
        value = f.total[g, pl.ds(pl.multiple_of(cz * f.block, f.block), f.block), :]
        for k in range(1, planes):
            value = value + f.zr[g, k - 1].astype(F32)
        out[:, g * 2 * f.half : (g + 1) * 2 * f.half] = value / total_rows

    def act_products():
        finish_gather(fa)
        choose(fa)
        far_part(fa, 0)
        near_part(fa, 0, 0)
        near_part(fa, 0, 1)
        own_part(fa, 0)
        relay_part(fa, 0)

    gain = gain_ref[...]
    scales = scale_ref[...]

    @pl.when(sec > 0)
    def _():
        build_picks()
        for j in range(chunks):
            load_in[j].wait()
            load_out[j].wait()
        for copy in forward_copies:
            copy.wait_recv()

    @pl.when(sec == 0)
    def _():
        load_x.wait()

    floats = x_in[...].reshape(tokens, width).astype(F32)
    center = floats - jnp.mean(floats, axis=-1, keepdims=True)
    inverse = lax.rsqrt(jnp.mean(center * center, axis=-1, keepdims=True) + 1e-06)
    normal = center * inverse
    normed[...] = normal
    inv_std[...] = inverse
    half_a = width // HALVES
    scaled_rows = (normal * gain).astype(BF16)
    for h in range(HALVES):
        rows_a[h, p] = scaled_rows[:, h * half_a : (h + 1) * half_a]

    def forward_chunk(j, scaled):
        cols = slice(j * chunk, (j + 1) * chunk)
        hidden = jnp.dot(scaled, win[:, cols], preferred_element_type=F32)
        cdf = 0.5 * (1.0 + lax.erf(hidden * SQRT_HALF))
        activated = (hidden * cdf).astype(BF16)
        slope[:, cols] = cdf + hidden * INV_ROOT_TAU * jnp.exp(-0.5 * hidden * hidden)
        part = jnp.dot(activated, wout[cols, :], preferred_element_type=F32)
        if j:
            accum[...] += part
        else:
            accum[...] = part

    @pl.when(sec == 0)
    def _():
        scaled = jnp.concatenate([rows_a[h, p] for h in range(HALVES)], axis=1)
        for j in range(chunks):
            load_in[j].wait()
            load_out[j].wait()
            forward_chunk(j, scaled)

    @pl.when(sec > 0)
    def _():
        scaled = jnp.concatenate([rows_a[h, p] for h in range(HALVES)], axis=1)
        for j in range(chunks):
            forward_chunk(j, scaled)

    pl.semaphore_wait(barrier, len(greeted))

    @pl.when(sec < sections - 1)
    def _():
        for m in range(batches):
            part = slice(m * rows, (m + 1) * rows)
            y_out[m] = (x_in[m].astype(F32) + scales * accum[part, :]).astype(BF16)
            forward_copies[m].start()

    for h in range(HALVES):
        start_half(fa, h)

    @pl.when(sec == 0)
    def _():
        build_picks()

    @pl.when(sec < sections // 2)
    def _():
        act_products()
        collect(fa, 0)

    @pl.when(sec < sections - 1)
    def _():
        for copy in backward_copies:
            copy.wait_recv()

    @pl.when(sec == sections - 1)
    def _():
        load_top.wait()

    def backward_chunk(j, gz, onward):
        cols = slice(j * chunk, (j + 1) * chunk)
        grad_act = lax.dot_general(gz, wout[cols, :], NT, preferred_element_type=F32)
        grad_hidden = (grad_act * slope[:, cols]).astype(BF16)
        per = chunks // HALVES
        h, inner = j // per, j % per
        rows_g[h, p, :, inner * chunk : (inner + 1) * chunk] = grad_hidden
        if onward:
            part = lax.dot_general(grad_hidden, win[:, cols], NT, preferred_element_type=F32)
            if j:
                accum[...] += part
            else:
                accum[...] = part
        if inner == per - 1:
            start_half(fg, h)

    @pl.when(sec == 0)
    def _():
        gz = (g_in[...].reshape(tokens, width).astype(F32) * scales).astype(BF16)
        for j in range(chunks):
            backward_chunk(j, gz, False)

    @pl.when(sec > 0)
    def _():
        gz = (g_in[...].reshape(tokens, width).astype(F32) * scales).astype(BF16)
        for j in range(chunks):
            backward_chunk(j, gz, True)
        for m in range(batches):
            part = slice(m * rows, (m + 1) * rows)
            normal_part = normed[part, :]
            grad_normed = accum[part, :] * gain
            mean_one = jnp.mean(grad_normed, axis=-1, keepdims=True)
            mean_two = jnp.mean(grad_normed * normal_part, axis=-1, keepdims=True)
            grad_input = g_in[m].astype(F32) + inv_std[part, :] * (
                grad_normed - mean_one - normal_part * mean_two
            )
            g_out[m] = grad_input.astype(BF16)
            backward_copies[m].start()

    finish_gather(fg)
    choose(fg)
    far_part(fg, 0)
    near_part(fg, 0, 0)
    near_part(fg, 0, 1)
    far_part(fg, 1)
    relay_part(fg, 0)
    near_part(fg, 1, 0)
    near_part(fg, 1, 1)
    own_part(fg, 0)
    relay_part(fg, 1)
    own_part(fg, 1)
    collect(fg, 0)

    @pl.when(sec >= sections // 2)
    def _():
        act_products()
        collect(fa, 0)

    collect(fg, 1)
    finish(fa, 0, act_ref)
    finish(fg, 0, grad_ref)
    finish(fg, 1, grad_ref)

    @pl.when(sec < sections - 1)
    def _():
        for copy in forward_copies:
            copy.wait_send()

    @pl.when(sec > 0)
    def _():
        for copy in backward_copies:
            copy.wait_send()

    for f in (fa, fg):
        for copy in f.gathers:
            copy.wait_send()
        for g in range(f.groups):
            for d in range(2):
                f.far_copy[g][d].wait_send()
                for h in range(2):
                    f.near_copy[g][d][h].wait_send()
            for copy in f.z_copy[g]:
                copy.wait_send()


def body(dp_count, sections, inputs, ln_gain, w_in, w_out, layer_scale, out_grad, owner_table):
    batches, rows, width = inputs.shape
    hidden_width = w_in.shape[2]
    planes = dp_count // (RING * RING)
    block_a = width // dp_count
    block_g = hidden_width // dp_count
    tokens = batches * rows
    chunk = min(256, hidden_width // HALVES)
    dma = pltpu.SemaphoreType.DMA
    vmem = pl.BlockSpec(memory_space=pltpu.VMEM)
    hbm = pl.BlockSpec(memory_space=pl.ANY)

    def factor_scratch(block, extent, groups):
        span = planes * block
        half = extent // groups // 2
        others = max(planes - 1, 1)
        return [
            pltpu.VMEM((RING * span, extent), BF16),
            pltpu.VMEM((HALVES, RING, tokens, extent // HALVES), BF16),
            pltpu.VMEM((RING * span, RING * tokens), BF16),
            pltpu.VMEM((groups, 2, span, half), BF16),
            pltpu.VMEM((groups, 2, 2, span, half), BF16),
            pltpu.VMEM((groups, 2, span, half), F32),
            pltpu.VMEM((groups, span, 2 * half), F32),
            pltpu.VMEM((groups, 2, span, half), BF16),
            pltpu.VMEM((groups, 2, 2, span, half), BF16),
            pltpu.VMEM((groups, others, block, 2 * half), BF16),
            pltpu.VMEM((groups, others, block, 2 * half), BF16),
        ]

    act, grad = pl.pallas_call(
        functools.partial(kernel, dp_count, sections),
        out_shape=(
            jax.ShapeDtypeStruct((block_a, width), F32),
            jax.ShapeDtypeStruct((block_g, hidden_width), F32),
        ),
        in_specs=[pl.BlockSpec(memory_space=pltpu.SMEM), hbm, hbm, vmem, vmem, hbm, hbm],
        out_specs=(vmem, vmem),
        scratch_shapes=[
            pltpu.VMEM((width, hidden_width), BF16),
            pltpu.VMEM((hidden_width, width), BF16),
            pltpu.VMEM((batches, rows, width), BF16),
            pltpu.VMEM((batches, rows, width), BF16),
            pltpu.VMEM((batches, rows, width), BF16),
            pltpu.VMEM((batches, rows, width), BF16),
            pltpu.VMEM((tokens, width), F32),
            pltpu.VMEM((tokens, 1), F32),
            pltpu.VMEM((tokens, hidden_width), F32),
            pltpu.VMEM((tokens, width), F32),
        ]
        + factor_scratch(block_a, width, 1)
        + factor_scratch(block_g, hidden_width, 2)
        + [
            dma((2, hidden_width // chunk)),
            dma((2,)),
            dma((2 * batches,)),
            dma((2 * batches,)),
            dma((2, 6)),
            dma((2, 6)),
            dma((2, 2, 6)),
            dma((2, 2, 6)),
            dma((2, 2, max(planes - 1, 1))),
            dma((2, 2, max(planes - 1, 1))),
        ],
        compiler_params=pltpu.CompilerParams(
            collective_id=0, has_side_effects=True, vmem_limit_bytes=60 * 1024 * 1024
        ),
        name="window",
    )(owner_table, inputs, out_grad, ln_gain, layer_scale, w_in[0], w_out[0])
    return (act[None], grad[None])


def solution(mesh):
    placed = (
        P(None, "dp", None),
        P("section", None),
        P("section", None, None),
        P("section", None, None),
        P("section", None),
        P(None, "dp", None),
        P(),
    )
    return jax.shard_map(
        functools.partial(body, mesh.shape["dp"], mesh.shape["section"]),
        mesh=mesh,
        in_specs=placed,
        out_specs=(P("section", "dp", None), P("section", "dp", None)),
        check_vma=False,
    )
```

```python
import functools
import jax
import jax.numpy as jnp
from jax import lax
from jax.experimental import pallas as pl
from jax.experimental.pallas import tpu as pltpu
from jax.sharding import PartitionSpec as P

SQRT_HALF = 0.7071067811865476
INV_ROOT_TAU = 0.3989422804014327
MESH = pl.DeviceIdType.MESH
F32 = jnp.float32
BF16 = jnp.bfloat16
NT = (((1,), (1,)), ((), ()))


RING = 4
HALVES = 2


def kernel(
    dp_count,
    sections,
    owner_ref,
    x_hbm,
    top_hbm,
    gain_ref,
    scale_ref,
    win_hbm,
    wout_hbm,
    act_ref,
    grad_ref,
    win,
    wout,
    x_in,
    y_out,
    g_in,
    g_out,
    normed,
    inv_std,
    slope,
    accum,
    acted,
    *rest,
):
    (pick_a, rows_a, left_a, far_a, near_a, hold_a, sum_a, far_in_a, near_in_a, zs_a, zr_a) = rest[:11]
    (pick_g, rows_g, left_g, far_g, near_g, hold_g, sum_g, far_in_g, near_in_g, zs_g, zr_g) = rest[11:22]
    (w_sem, io_sem, relay_s, relay_r, gat_s, gat_r, sca_s, sca_r, z_s, z_r) = rest[22:]
    planes = dp_count // (RING * RING)
    sec = lax.axis_index("section")
    me = lax.axis_index("dp")
    cx = me // (planes * RING)
    cz = lax.rem(me // RING, planes)
    cy = lax.rem(me, RING)
    even = lax.rem(sec, 2) == 0
    _, batches, rows, half_width = x_in.shape
    width = HALVES * half_width
    tokens = batches * rows
    hidden_width = win.shape[1]
    block_a = width // dp_count
    block_g = hidden_width // dp_count
    chunk = min(256, hidden_width // HALVES)
    chunks = hidden_width // chunk

    def index_of(px, pz, py):
        return px * planes * RING + pz * RING + py

    p = jnp.where(even, cx, cy)
    q = jnp.where(even, cy, cx)

    def at_pq(pp, pz, qq):
        return index_of(jnp.where(even, pp, qq), pz, jnp.where(even, qq, pp))

    def ring(value, k):
        return lax.rem(value + k + RING, RING)

    def p_peer(k):
        return (at_pq(ring(p, k), cz, q), sec)

    def q_peer(k):
        return (at_pq(p, cz, ring(q, k)), sec)

    def z_peer(k):
        return (index_of(cx, lax.rem(cz + k, planes), cy), sec)

    def remote(src, dst, ssem, rsem, device):
        return pltpu.make_async_remote_copy(
            src_ref=src, dst_ref=dst, send_sem=ssem, recv_sem=rsem,
            device_id=device, device_id_type=MESH,
        )

    load_in = []
    load_out = []
    for j in range(chunks):
        cols = pl.ds(j * chunk, chunk)
        load_in.append(pltpu.make_async_copy(win_hbm.at[:, cols], win.at[:, cols], w_sem.at[0, j]))
        load_out.append(pltpu.make_async_copy(wout_hbm.at[cols, :], wout.at[cols, :], w_sem.at[1, j]))
    load_x = []
    load_top = []
    for h in range(HALVES):
        cols = pl.ds(h * half_width, half_width)
        for m in range(batches):
            load_x.append(
                pltpu.make_async_copy(x_hbm.at[m, :, cols], x_in.at[h, m], io_sem.at[0, h * batches + m])
            )
            load_top.append(
                pltpu.make_async_copy(top_hbm.at[m, :, cols], g_in.at[h, m], io_sem.at[1, h * batches + m])
            )

    @pl.when(sec == 0)
    def _():
        for copy in load_x:
            copy.start()

    for copy in load_in + load_out:
        copy.start()

    @pl.when(sec == sections - 1)
    def _():
        for copy in load_top:
            copy.start()

    barrier = pltpu.get_barrier_semaphore()
    greeted = [p_peer(1), p_peer(-1), q_peer(1), q_peer(-1)]
    greeted += [z_peer(k) for k in range(1, planes)]
    greeted += [(me, lax.rem(sec + 1, sections)), (me, lax.rem(sec + sections - 1, sections))]
    for device in greeted:
        pl.semaphore_signal(barrier, inc=1, device_id=device, device_id_type=MESH)

    def build_picks():
        for pick, block in ((pick_a, block_a), (pick_g, block_g)):
            extent = pick.shape[1]
            offset = lax.broadcasted_iota(jnp.int32, (block, extent), 1) - lax.broadcasted_iota(
                jnp.int32, (block, extent), 0
            )
            for qq in range(RING):
                for zz in range(planes):
                    owner = owner_ref[at_pq(p, zz, qq)]
                    row = (qq * planes + zz) * block
                    pick[row : row + block, :] = jnp.where(offset == owner * block, 1.0, 0.0).astype(BF16)

    forward_copies = [
        remote(y_out.at[h], x_in.at[h], relay_s.at[h], relay_r.at[h], (me, lax.rem(sec + 1, sections)))
        for h in range(HALVES)
    ]
    backward_copies = [
        remote(
            g_out.at[h], g_in.at[h], relay_s.at[HALVES + h], relay_r.at[HALVES + h],
            (me, lax.rem(sec + sections - 1, sections)),
        )
        for h in range(HALVES)
    ]

    class Factor:
        pass

    def factor(number, block, groups, pick, buffers):
        f = Factor()
        f.block, f.span, f.groups, f.pick = block, planes * block, groups, pick
        (f.rows, f.left, f.far, f.near, f.hold, f.total, f.far_in, f.near_in, f.zs, f.zr) = buffers
        f.half = f.far.shape[3]
        gs, gr = gat_s.at[number], gat_r.at[number]

        def row_copy(slot, h, part, n, k):
            piece = f.rows.at[h, slot]
            if part is not None:
                piece = f.rows.at[h, slot, pl.ds(part * (tokens // 2), tokens // 2)]
            return remote(piece, piece, gs.at[n], gr.at[n], p_peer(k))

        before, after = ring(p, -1), ring(p, 1)
        f.plus = [row_copy(p, 0, None, 0, 1), row_copy(p, 1, None, 1, 1), row_copy(before, 0, None, 2, 1)]
        f.minus = [row_copy(p, 0, None, 3, -1)]
        f.minus += [row_copy(p, 1, i, 4 + i, -1) for i in range(2)]
        f.minus += [row_copy(after, 1, i, 6 + i, -1) for i in range(2)]
        f.gathers = f.plus + f.minus
        ss, sr = sca_s.at[number], sca_r.at[number]
        f.far_copy = [
            [
                remote(f.far.at[g, d], f.far_in.at[g, d], ss.at[g, d], sr.at[g, d], q_peer((1, -1)[d]))
                for d in range(2)
            ]
            for g in range(groups)
        ]
        f.near_copy = [
            [
                [
                    remote(
                        f.near.at[g, d, h], f.near_in.at[g, d, h], ss.at[g, 2 + 2 * d + h],
                        sr.at[g, 2 + 2 * d + h], q_peer((1, -1)[d]),
                    )
                    for h in range(2)
                ]
                for d in range(2)
            ]
            for g in range(groups)
        ]
        f.z_copy = [
            [
                remote(
                    f.zs.at[g, k - 1], f.zr.at[g, k - 1], z_s.at[number, g, k - 1],
                    z_r.at[number, g, k - 1], z_peer(k),
                )
                for k in range(1, planes)
            ]
            for g in range(groups)
        ]
        return f

    fa = factor(0, block_a, 1, pick_a, (rows_a, left_a, far_a, near_a, hold_a, sum_a, far_in_a, near_in_a, zs_a, zr_a))
    fg = factor(1, block_g, 2, pick_g, (rows_g, left_g, far_g, near_g, hold_g, sum_g, far_in_g, near_in_g, zs_g, zr_g))

    def start_half(f, h):
        f.plus[h].start()
        if h == 0:
            f.minus[0].start()
        else:
            f.minus[1].start()
            f.minus[2].start()

    def choose(f, sources):
        extent = f.rows.shape[3]
        picked = None
        for h in range(HALVES):
            pieces = [f.rows[h, source] for source in sources]
            piece = pieces[0] if len(pieces) == 1 else jnp.concatenate(pieces, axis=0)
            part = lax.dot_general(
                f.pick[:, h * extent : (h + 1) * extent], piece, NT, preferred_element_type=F32
            )
            picked = part if picked is None else picked + part
        for i, source in enumerate(sources):
            f.left[:, pl.ds(pl.multiple_of(source * tokens, tokens), tokens)] = picked[
                :, i * tokens : (i + 1) * tokens
            ].astype(BF16)

    def finish_gather(f):
        choose(f, [p])
        f.plus[0].wait_recv()
        f.plus[2].start()
        f.minus[1].wait_recv()
        f.minus[3].start()
        f.minus[2].wait_recv()
        f.minus[4].start()
        f.plus[1].wait_recv()
        f.minus[0].wait_recv()
        choose(f, [ring(p, -1), ring(p, 1)])
        f.plus[2].wait_recv()
        f.minus[3].wait_recv()
        f.minus[4].wait_recv()
        choose(f, [ring(p, 2)])

    def part_of(f, g, k):
        extent = f.rows.shape[3]
        dest = ring(q, k)
        left = f.left[pl.ds(pl.multiple_of(dest * f.span, f.span), f.span), :]
        pieces = [
            jnp.dot(left, f.rows[h].reshape(RING * tokens, extent), preferred_element_type=F32)
            for h in ((g,) if f.groups == 2 else range(HALVES))
        ]
        return pieces[0] if len(pieces) == 1 else jnp.concatenate(pieces, axis=1)

    def far_part(f, g):
        part = part_of(f, g, 2)
        for d in range(2):
            f.far[g, d] = part[:, d * f.half : (d + 1) * f.half].astype(BF16)
            f.far_copy[g][d].start()

    def near_part(f, g, d):
        part = part_of(f, g, (1, -1)[d])
        free = 1 - d
        f.near[g, d, free] = part[:, free * f.half : (free + 1) * f.half].astype(BF16)
        f.near_copy[g][d][free].start()
        f.hold[g, d] = part[:, d * f.half : (d + 1) * f.half]

    def own_part(f, g):
        f.total[g] = part_of(f, g, 0)

    def relay_part(f, g):
        for d in range(2):
            f.far_copy[g][d].wait_recv()
            f.near[g, d, d] = (f.hold[g, d] + f.far_in[g, d].astype(F32)).astype(BF16)
            f.near_copy[g][d][d].start()

    def collect(f, g):
        for d in range(2):
            for h in range(2):
                f.near_copy[g][d][h].wait_recv()
        for h in range(2):
            cols = slice(h * f.half, (h + 1) * f.half)
            f.total[g, :, cols] += f.near_in[g, 0, h].astype(F32) + f.near_in[g, 1, h].astype(F32)
        for k in range(1, planes):
            dest = lax.rem(cz + k, planes)
            f.zs[g, k - 1] = f.total[g, pl.ds(pl.multiple_of(dest * f.block, f.block), f.block), :].astype(BF16)
            f.z_copy[g][k - 1].start()

    def finish(f, g, out):
        for copy in f.z_copy[g]:
            copy.wait_recv()
        value = f.total[g, pl.ds(pl.multiple_of(cz * f.block, f.block), f.block), :]
        for k in range(1, planes):
            value = value + f.zr[g, k - 1].astype(F32)
        out[:, g * 2 * f.half : (g + 1) * 2 * f.half] = value

    def act_products():
        finish_gather(fa)
        far_part(fa, 0)
        near_part(fa, 0, 0)
        near_part(fa, 0, 1)
        own_part(fa, 0)
        relay_part(fa, 0)

    gain = gain_ref[...]
    scales = scale_ref[...]

    @pl.when(sec > 0)
    def _():
        build_picks()
        for copy in load_in + load_out:
            copy.wait()
        for copy in forward_copies:
            copy.wait_recv()

    @pl.when(sec == 0)
    def _():
        for copy in load_x:
            copy.wait()

    def joined(ref):
        return jnp.concatenate([ref[h].reshape(tokens, half_width) for h in range(HALVES)], axis=1)

    floats = joined(x_in).astype(F32)
    center = floats - jnp.mean(floats, axis=-1, keepdims=True)
    inverse = lax.rsqrt(jnp.mean(center * center, axis=-1, keepdims=True) + 1e-06)
    normal = center * inverse
    normed[...] = normal
    inv_std[...] = inverse
    scaled_rows = (normal * gain).astype(BF16)
    for h in range(HALVES):
        rows_a[h, p] = scaled_rows[:, h * half_width : (h + 1) * half_width]

    def forward_chunk(j, scaled):
        cols = slice(j * chunk, (j + 1) * chunk)
        hidden = jnp.dot(scaled, win[:, cols], preferred_element_type=F32)
        cdf = 0.5 * (1.0 + lax.erf(hidden * SQRT_HALF))
        acted[:, cols] = (hidden * cdf).astype(BF16)
        slope[:, cols] = cdf + hidden * INV_ROOT_TAU * jnp.exp(-0.5 * hidden * hidden)

    @pl.when(sec == 0)
    def _():
        scaled = jnp.concatenate([rows_a[h, p] for h in range(HALVES)], axis=1)
        for j in range(chunks):
            load_in[j].wait()
            forward_chunk(j, scaled)
        for copy in load_out:
            copy.wait()

    @pl.when(sec > 0)
    def _():
        scaled = jnp.concatenate([rows_a[h, p] for h in range(HALVES)], axis=1)
        for j in range(chunks):
            forward_chunk(j, scaled)

    pl.semaphore_wait(barrier, len(greeted))

    @pl.when(sec < sections - 1)
    def _():
        values = acted[...]
        for h in range(HALVES):
            cols = slice(h * half_width, (h + 1) * half_width)
            part = jnp.dot(values, wout[:, cols], preferred_element_type=F32)
            output = x_in[h].reshape(tokens, half_width).astype(F32) + scales[:, cols] * part
            y_out[h] = output.astype(BF16).reshape(batches, rows, half_width)
            forward_copies[h].start()

    for h in range(HALVES):
        start_half(fa, h)

    @pl.when(sec == 0)
    def _():
        build_picks()

    @pl.when(sec < sections // 2)
    def _():
        act_products()
        collect(fa, 0)

    @pl.when(sec < sections - 1)
    def _():
        for copy in backward_copies:
            copy.wait_recv()

    @pl.when(sec == sections - 1)
    def _():
        for copy in load_top:
            copy.wait()

    cotangent = joined(g_in).astype(F32)
    gz = (cotangent * scales).astype(BF16)
    per = chunks // HALVES
    for j in range(chunks):
        cols = slice(j * chunk, (j + 1) * chunk)
        grad_act = lax.dot_general(gz, wout[cols, :], NT, preferred_element_type=F32)
        h, inner = j // per, j % per
        rows_g[h, p, :, inner * chunk : (inner + 1) * chunk] = (grad_act * slope[:, cols]).astype(BF16)
        if inner == per - 1:
            start_half(fg, h)

    @pl.when(sec > 0)
    def _():
        grad_hidden = jnp.concatenate([rows_g[h, p] for h in range(HALVES)], axis=1)
        for h in range(HALVES):
            cols = slice(h * half_width, (h + 1) * half_width)
            accum[:, cols] = lax.dot_general(
                grad_hidden, win[cols, :], NT, preferred_element_type=F32
            )
        normal = normed[...]
        grad_normed = accum[...] * gain
        mean_one = jnp.mean(grad_normed, axis=-1, keepdims=True)
        mean_two = jnp.mean(grad_normed * normal, axis=-1, keepdims=True)
        scale_back = inv_std[...]
        for h in range(HALVES):
            cols = slice(h * half_width, (h + 1) * half_width)
            grad_input = g_in[h].reshape(tokens, half_width).astype(F32) + scale_back * (
                accum[:, cols] * gain[:, cols] - mean_one - normed[:, cols] * mean_two
            )
            g_out[h] = grad_input.astype(BF16).reshape(batches, rows, half_width)
            backward_copies[h].start()

    finish_gather(fg)
    far_part(fg, 0)
    near_part(fg, 0, 0)
    near_part(fg, 0, 1)
    far_part(fg, 1)
    relay_part(fg, 0)
    near_part(fg, 1, 0)
    near_part(fg, 1, 1)
    own_part(fg, 0)
    relay_part(fg, 1)
    own_part(fg, 1)
    collect(fg, 0)

    @pl.when(sec >= sections // 2)
    def _():
        act_products()
        collect(fa, 0)

    collect(fg, 1)
    finish(fa, 0, act_ref)
    finish(fg, 0, grad_ref)
    finish(fg, 1, grad_ref)

    @pl.when(sec < sections - 1)
    def _():
        for copy in forward_copies:
            copy.wait_send()

    @pl.when(sec > 0)
    def _():
        for copy in backward_copies:
            copy.wait_send()

    for f in (fa, fg):
        for copy in f.gathers:
            copy.wait_send()
        for g in range(f.groups):
            for d in range(2):
                f.far_copy[g][d].wait_send()
                for h in range(2):
                    f.near_copy[g][d][h].wait_send()
            for copy in f.z_copy[g]:
                copy.wait_send()


def scale_kernel(factor, act_ref, grad_ref, act_out, grad_out):
    act_out[0] = act_ref[...] * factor
    grad_out[0] = grad_ref[...] * factor


def body(dp_count, sections, inputs, ln_gain, w_in, w_out, layer_scale, out_grad, owner_table):
    batches, rows, width = inputs.shape
    hidden_width = w_in.shape[2]
    planes = dp_count // (RING * RING)
    block_a = width // dp_count
    block_g = hidden_width // dp_count
    tokens = batches * rows
    chunk = min(256, hidden_width // HALVES)
    dma = pltpu.SemaphoreType.DMA
    vmem = pl.BlockSpec(memory_space=pltpu.VMEM)
    hbm = pl.BlockSpec(memory_space=pl.ANY)

    def factor_scratch(block, extent, groups):
        span = planes * block
        half = extent // groups // 2
        others = max(planes - 1, 1)
        return [
            pltpu.VMEM((RING * span, extent), BF16),
            pltpu.VMEM((HALVES, RING, tokens, extent // HALVES), BF16),
            pltpu.VMEM((RING * span, RING * tokens), BF16),
            pltpu.VMEM((groups, 2, span, half), BF16),
            pltpu.VMEM((groups, 2, 2, span, half), BF16),
            pltpu.VMEM((groups, 2, span, half), F32),
            pltpu.VMEM((groups, span, 2 * half), F32),
            pltpu.VMEM((groups, 2, span, half), BF16),
            pltpu.VMEM((groups, 2, 2, span, half), BF16),
            pltpu.VMEM((groups, others, block, 2 * half), BF16),
            pltpu.VMEM((groups, others, block, 2 * half), BF16),
        ]

    act, grad = pl.pallas_call(
        functools.partial(kernel, dp_count, sections),
        out_shape=(
            jax.ShapeDtypeStruct((block_a, width), F32),
            jax.ShapeDtypeStruct((block_g, hidden_width), F32),
        ),
        in_specs=[pl.BlockSpec(memory_space=pltpu.SMEM), hbm, hbm, vmem, vmem, hbm, hbm],
        out_specs=(vmem, vmem),
        scratch_shapes=[
            pltpu.VMEM((width, hidden_width), BF16),
            pltpu.VMEM((hidden_width, width), BF16),
            pltpu.VMEM((HALVES, batches, rows, width // HALVES), BF16),
            pltpu.VMEM((HALVES, batches, rows, width // HALVES), BF16),
            pltpu.VMEM((HALVES, batches, rows, width // HALVES), BF16),
            pltpu.VMEM((HALVES, batches, rows, width // HALVES), BF16),
            pltpu.VMEM((tokens, width), F32),
            pltpu.VMEM((tokens, 1), F32),
            pltpu.VMEM((tokens, hidden_width), F32),
            pltpu.VMEM((tokens, width), F32),
            pltpu.VMEM((tokens, hidden_width), BF16),
        ]
        + factor_scratch(block_a, width, 1)
        + factor_scratch(block_g, hidden_width, 2)
        + [
            dma((2, hidden_width // chunk)),
            dma((2, HALVES * batches)),
            dma((2 * HALVES,)),
            dma((2 * HALVES,)),
            dma((2, 8)),
            dma((2, 8)),
            dma((2, 2, 6)),
            dma((2, 2, 6)),
            dma((2, 2, max(planes - 1, 1))),
            dma((2, 2, max(planes - 1, 1))),
        ],
        compiler_params=pltpu.CompilerParams(
            collective_id=0, has_side_effects=True, vmem_limit_bytes=60 * 1024 * 1024
        ),
        name="window",
    )(owner_table, inputs, out_grad, ln_gain, layer_scale, w_in[0], w_out[0])
    factor = 1.0 / (tokens * dp_count)
    return pl.pallas_call(
        functools.partial(scale_kernel, factor),
        out_shape=(
            jax.ShapeDtypeStruct((1, block_a, width), F32),
            jax.ShapeDtypeStruct((1, block_g, hidden_width), F32),
        ),
        in_specs=[vmem, vmem],
        out_specs=(vmem, vmem),
        compiler_params=pltpu.CompilerParams(vmem_limit_bytes=60 * 1024 * 1024),
        name="mean",
    )(act, grad)


def solution(mesh):
    placed = (
        P(None, "dp", None),
        P("section", None),
        P("section", None, None),
        P("section", None, None),
        P("section", None),
        P(None, "dp", None),
        P(),
    )
    return jax.shard_map(
        functools.partial(body, mesh.shape["dp"], mesh.shape["section"]),
        mesh=mesh,
        in_specs=placed,
        out_specs=(P("section", "dp", None), P("section", "dp", None)),
        check_vma=False,
    )
```

```python
import functools
import jax
import jax.numpy as jnp
from jax import lax
from jax.experimental import pallas as pl
from jax.experimental.pallas import tpu as pltpu
from jax.sharding import PartitionSpec as P

SQRT_HALF = 0.7071067811865476
INV_ROOT_TAU = 0.3989422804014327
MESH = pl.DeviceIdType.MESH
F32 = jnp.float32
BF16 = jnp.bfloat16
NT = (((1,), (1,)), ((), ()))


RING = 4
HALVES = 2


def kernel(
    dp_count,
    sections,
    owner_ref,
    x_hbm,
    top_hbm,
    gain_ref,
    scale_ref,
    win_hbm,
    wout_hbm,
    act_ref,
    grad_ref,
    win,
    wout,
    x_in,
    y_out,
    g_in,
    g_out,
    normed,
    inv_std,
    slope,
    accum,
    acted,
    win_t,
    wout_t,
    *rest,
):
    (pick_a, rows_a, left_a, far_a, near_a, hold_a, sum_a, far_in_a, near_in_a, zs_a, zr_a) = rest[:11]
    (pick_g, rows_g, left_g, far_g, near_g, hold_g, sum_g, far_in_g, near_in_g, zs_g, zr_g) = rest[11:22]
    (w_sem, io_sem, relay_s, relay_r, gat_s, gat_r, sca_s, sca_r, z_s, z_r, turn) = rest[22:]
    planes = dp_count // (RING * RING)
    sec = lax.axis_index("section")
    me = lax.axis_index("dp")
    cx = me // (planes * RING)
    cz = lax.rem(me // RING, planes)
    cy = lax.rem(me, RING)
    even = lax.rem(sec, 2) == 0
    _, batches, rows, half_width = x_in.shape
    width = HALVES * half_width
    tokens = batches * rows
    hidden_width = win.shape[1]
    block_a = width // dp_count
    block_g = hidden_width // dp_count
    chunk = min(256, hidden_width // HALVES)
    chunks = hidden_width // chunk

    def index_of(px, pz, py):
        return px * planes * RING + pz * RING + py

    p = jnp.where(even, cx, cy)
    q = jnp.where(even, cy, cx)

    def at_pq(pp, pz, qq):
        return index_of(jnp.where(even, pp, qq), pz, jnp.where(even, qq, pp))

    def ring(value, k):
        return lax.rem(value + k + RING, RING)

    def p_peer(k):
        return (at_pq(ring(p, k), cz, q), sec)

    def q_peer(k):
        return (at_pq(p, cz, ring(q, k)), sec)

    def z_peer(k):
        return (index_of(cx, lax.rem(cz + k, planes), cy), sec)

    def remote(src, dst, ssem, rsem, device):
        return pltpu.make_async_remote_copy(
            src_ref=src, dst_ref=dst, send_sem=ssem, recv_sem=rsem,
            device_id=device, device_id_type=MESH,
        )

    load_in = []
    load_out = []
    for j in range(chunks):
        cols = pl.ds(j * chunk, chunk)
        load_in.append(pltpu.make_async_copy(win_hbm.at[:, cols], win.at[:, cols], w_sem.at[0, j]))
        load_out.append(pltpu.make_async_copy(wout_hbm.at[cols, :], wout.at[cols, :], w_sem.at[1, j]))
    load_x = []
    load_top = []
    for h in range(HALVES):
        cols = pl.ds(h * half_width, half_width)
        for m in range(batches):
            load_x.append(
                pltpu.make_async_copy(x_hbm.at[m, :, cols], x_in.at[h, m], io_sem.at[0, h * batches + m])
            )
            load_top.append(
                pltpu.make_async_copy(top_hbm.at[m, :, cols], g_in.at[h, m], io_sem.at[1, h * batches + m])
            )

    @pl.when(sec == 0)
    def _():
        for copy in load_x:
            copy.start()

    for copy in load_in + load_out:
        copy.start()

    @pl.when(sec == sections - 1)
    def _():
        for copy in load_top:
            copy.start()

    barrier = pltpu.get_barrier_semaphore()
    greeted = [p_peer(1), p_peer(-1), q_peer(1), q_peer(-1)]
    greeted += [z_peer(k) for k in range(1, planes)]
    greeted += [(me, lax.rem(sec + 1, sections)), (me, lax.rem(sec + sections - 1, sections))]
    for device in greeted:
        pl.semaphore_signal(barrier, inc=1, device_id=device, device_id_type=MESH)

    def build_picks():
        for pick, block in ((pick_a, block_a), (pick_g, block_g)):
            extent = pick.shape[1]
            offset = lax.broadcasted_iota(jnp.int32, (block, extent), 1) - lax.broadcasted_iota(
                jnp.int32, (block, extent), 0
            )
            for qq in range(RING):
                for zz in range(planes):
                    owner = owner_ref[at_pq(p, zz, qq)]
                    row = (qq * planes + zz) * block
                    pick[row : row + block, :] = jnp.where(offset == owner * block, 1.0, 0.0).astype(BF16)

    forward_copies = [
        remote(y_out.at[h], x_in.at[h], relay_s.at[h], relay_r.at[h], (me, lax.rem(sec + 1, sections)))
        for h in range(HALVES)
    ]
    backward_copies = [
        remote(
            g_out.at[h], g_in.at[h], relay_s.at[HALVES + h], relay_r.at[HALVES + h],
            (me, lax.rem(sec + sections - 1, sections)),
        )
        for h in range(HALVES)
    ]

    class Factor:
        pass

    def factor(number, block, groups, pick, buffers):
        f = Factor()
        f.block, f.span, f.groups, f.pick = block, planes * block, groups, pick
        (f.rows, f.left, f.far, f.near, f.hold, f.total, f.far_in, f.near_in, f.zs, f.zr) = buffers
        f.half = f.far.shape[3]
        gs, gr = gat_s.at[number], gat_r.at[number]

        def row_copy(slot, h, part, n, k):
            piece = f.rows.at[h, slot]
            if part is not None:
                piece = f.rows.at[h, slot, pl.ds(part * (tokens // 2), tokens // 2)]
            return remote(piece, piece, gs.at[n], gr.at[n], p_peer(k))

        before, after = ring(p, -1), ring(p, 1)
        f.plus = [row_copy(p, 0, None, 0, 1), row_copy(p, 1, None, 1, 1), row_copy(before, 0, None, 2, 1)]
        f.minus = [row_copy(p, 0, None, 3, -1)]
        f.minus += [row_copy(p, 1, i, 4 + i, -1) for i in range(2)]
        f.minus += [row_copy(after, 1, i, 6 + i, -1) for i in range(2)]
        f.gathers = f.plus + f.minus
        ss, sr = sca_s.at[number], sca_r.at[number]
        f.far_copy = [
            [
                remote(f.far.at[g, d], f.far_in.at[g, d], ss.at[g, d], sr.at[g, d], q_peer((1, -1)[d]))
                for d in range(2)
            ]
            for g in range(groups)
        ]
        f.near_copy = [
            [
                [
                    remote(
                        f.near.at[g, d, h], f.near_in.at[g, d, h], ss.at[g, 2 + 2 * d + h],
                        sr.at[g, 2 + 2 * d + h], q_peer((1, -1)[d]),
                    )
                    for h in range(2)
                ]
                for d in range(2)
            ]
            for g in range(groups)
        ]
        f.z_copy = [
            [
                remote(
                    f.zs.at[g, k - 1], f.zr.at[g, k - 1], z_s.at[number, g, k - 1],
                    z_r.at[number, g, k - 1], z_peer(k),
                )
                for k in range(1, planes)
            ]
            for g in range(groups)
        ]
        return f

    fa = factor(0, block_a, 1, pick_a, (rows_a, left_a, far_a, near_a, hold_a, sum_a, far_in_a, near_in_a, zs_a, zr_a))
    fg = factor(1, block_g, 2, pick_g, (rows_g, left_g, far_g, near_g, hold_g, sum_g, far_in_g, near_in_g, zs_g, zr_g))

    def start_half(f, h):
        f.plus[h].start()
        if h == 0:
            f.minus[0].start()
        else:
            f.minus[1].start()
            f.minus[2].start()

    def choose(f, sources):
        extent = f.rows.shape[3]
        picked = None
        for h in range(HALVES):
            pieces = [f.rows[h, source] for source in sources]
            piece = pieces[0] if len(pieces) == 1 else jnp.concatenate(pieces, axis=0)
            part = lax.dot_general(
                f.pick[:, h * extent : (h + 1) * extent], piece, NT, preferred_element_type=F32
            )
            picked = part if picked is None else picked + part
        for i, source in enumerate(sources):
            f.left[:, pl.ds(pl.multiple_of(source * tokens, tokens), tokens)] = picked[
                :, i * tokens : (i + 1) * tokens
            ].astype(BF16)

    def give_turn():
        @pl.when(even)
        def _():
            pl.semaphore_signal(turn, inc=1, device_id=(me, lax.rem(sec + 1, sections)), device_id_type=MESH)

    def take_turn():
        @pl.when(jnp.logical_not(even))
        def _():
            pl.semaphore_wait(turn, 1)

    def finish_gather(f):
        choose(f, [p])
        f.plus[0].wait_recv()
        f.plus[2].start()
        f.minus[1].wait_recv()
        f.minus[3].start()
        f.minus[2].wait_recv()
        f.minus[4].start()
        f.plus[1].wait_recv()
        f.minus[0].wait_recv()
        if f is fg:
            give_turn()
        choose(f, [ring(p, -1), ring(p, 1)])
        f.plus[2].wait_recv()
        f.minus[3].wait_recv()
        f.minus[4].wait_recv()
        choose(f, [ring(p, 2)])

    def part_of(f, g, k):
        extent = f.rows.shape[3]
        dest = ring(q, k)
        left = f.left[pl.ds(pl.multiple_of(dest * f.span, f.span), f.span), :]
        pieces = [
            jnp.dot(left, f.rows[h].reshape(RING * tokens, extent), preferred_element_type=F32)
            for h in ((g,) if f.groups == 2 else range(HALVES))
        ]
        return pieces[0] if len(pieces) == 1 else jnp.concatenate(pieces, axis=1)

    def far_part(f, g):
        part = part_of(f, g, 2)
        for d in range(2):
            f.far[g, d] = part[:, d * f.half : (d + 1) * f.half].astype(BF16)
            f.far_copy[g][d].start()

    def near_part(f, g, d):
        part = part_of(f, g, (1, -1)[d])
        free = 1 - d
        f.near[g, d, free] = part[:, free * f.half : (free + 1) * f.half].astype(BF16)
        f.near_copy[g][d][free].start()
        f.hold[g, d] = part[:, d * f.half : (d + 1) * f.half]

    def own_part(f, g):
        f.total[g] = part_of(f, g, 0)

    def relay_part(f, g):
        for d in range(2):
            f.far_copy[g][d].wait_recv()
            f.near[g, d, d] = (f.hold[g, d] + f.far_in[g, d].astype(F32)).astype(BF16)
            f.near_copy[g][d][d].start()

    def collect(f, g):
        for d in range(2):
            for h in range(2):
                f.near_copy[g][d][h].wait_recv()
        for h in range(2):
            cols = slice(h * f.half, (h + 1) * f.half)
            f.total[g, :, cols] += f.near_in[g, 0, h].astype(F32) + f.near_in[g, 1, h].astype(F32)
        for k in range(1, planes):
            dest = lax.rem(cz + k, planes)
            f.zs[g, k - 1] = f.total[g, pl.ds(pl.multiple_of(dest * f.block, f.block), f.block), :].astype(BF16)
            f.z_copy[g][k - 1].start()

    def finish(f, g, out):
        for copy in f.z_copy[g]:
            copy.wait_recv()
        value = f.total[g, pl.ds(pl.multiple_of(cz * f.block, f.block), f.block), :]
        for k in range(1, planes):
            value = value + f.zr[g, k - 1].astype(F32)
        out[:, g * 2 * f.half : (g + 1) * 2 * f.half] = value

    def act_products():
        finish_gather(fa)
        far_part(fa, 0)
        near_part(fa, 0, 0)
        near_part(fa, 0, 1)
        own_part(fa, 0)
        relay_part(fa, 0)

    def transpose_weights():
        for source, target in ((wout, wout_t), (win, win_t)):
            count = source.shape[0] // chunk

            def step(i, carry):
                at = pl.ds(pl.multiple_of(i * chunk, chunk), chunk)
                target[:, at] = source[at, :].T
                return carry

            lax.fori_loop(0, count, step, 0)

    gain = gain_ref[...]
    scales = scale_ref[...]

    @pl.when(sec > 0)
    def _():
        build_picks()
        for copy in load_in + load_out:
            copy.wait()

        @pl.when(sec == sections - 1)
        def _():
            transpose_weights()

        for copy in forward_copies:
            copy.wait_recv()

    @pl.when(sec == 0)
    def _():
        for copy in load_x:
            copy.wait()

    def joined(ref):
        return jnp.concatenate([ref[h].reshape(tokens, half_width) for h in range(HALVES)], axis=1)

    floats = joined(x_in).astype(F32)
    center = floats - jnp.mean(floats, axis=-1, keepdims=True)
    inverse = lax.rsqrt(jnp.mean(center * center, axis=-1, keepdims=True) + 1e-06)
    normal = center * inverse
    normed[...] = normal
    inv_std[...] = inverse
    scaled_rows = (normal * gain).astype(BF16)
    for h in range(HALVES):
        rows_a[h, p] = scaled_rows[:, h * half_width : (h + 1) * half_width]

    def forward_chunk(j, scaled):
        cols = slice(j * chunk, (j + 1) * chunk)
        hidden = jnp.dot(scaled, win[:, cols], preferred_element_type=F32)
        cdf = 0.5 * (1.0 + lax.erf(hidden * SQRT_HALF))
        acted[:, cols] = (hidden * cdf).astype(BF16)
        slope[:, cols] = cdf + hidden * INV_ROOT_TAU * jnp.exp(-0.5 * hidden * hidden)

    @pl.when(sec == 0)
    def _():
        scaled = jnp.concatenate([rows_a[h, p] for h in range(HALVES)], axis=1)
        for j in range(chunks):
            load_in[j].wait()
            forward_chunk(j, scaled)
        for copy in load_out:
            copy.wait()

    @pl.when(sec > 0)
    def _():
        scaled = jnp.concatenate([rows_a[h, p] for h in range(HALVES)], axis=1)
        for j in range(chunks):
            forward_chunk(j, scaled)

    pl.semaphore_wait(barrier, len(greeted))

    @pl.when(sec < sections - 1)
    def _():
        values = acted[...]
        for h in range(HALVES):
            cols = slice(h * half_width, (h + 1) * half_width)
            part = jnp.dot(values, wout[:, cols], preferred_element_type=F32)
            output = x_in[h].reshape(tokens, half_width).astype(F32) + scales[:, cols] * part
            y_out[h] = output.astype(BF16).reshape(batches, rows, half_width)
            forward_copies[h].start()

    for h in range(HALVES):
        start_half(fa, h)

    @pl.when(sec == 0)
    def _():
        build_picks()

    @pl.when(sec < sections - 1)
    def _():
        transpose_weights()

    @pl.when(sec < sections // 2)
    def _():
        act_products()
        collect(fa, 0)

    @pl.when(sec < sections - 1)
    def _():
        for copy in backward_copies:
            copy.wait_recv()

    @pl.when(sec == sections - 1)
    def _():
        for copy in load_top:
            copy.wait()

    cotangent = joined(g_in).astype(F32)
    gz = (cotangent * scales).astype(BF16)
    per = chunks // HALVES
    for j in range(chunks):
        cols = slice(j * chunk, (j + 1) * chunk)
        grad_act = jnp.dot(gz, wout_t[:, cols], preferred_element_type=F32)
        h, inner = j // per, j % per
        rows_g[h, p, :, inner * chunk : (inner + 1) * chunk] = (grad_act * slope[:, cols]).astype(BF16)
        if inner == per - 1:
            start_half(fg, h)

    @pl.when(sec > 0)
    def _():
        grad_hidden = jnp.concatenate([rows_g[h, p] for h in range(HALVES)], axis=1)
        for h in range(HALVES):
            cols = slice(h * half_width, (h + 1) * half_width)
            accum[:, cols] = jnp.dot(grad_hidden, win_t[:, cols], preferred_element_type=F32)
        normal = normed[...]
        grad_normed = accum[...] * gain
        mean_one = jnp.mean(grad_normed, axis=-1, keepdims=True)
        mean_two = jnp.mean(grad_normed * normal, axis=-1, keepdims=True)
        scale_back = inv_std[...]
        for h in range(HALVES):
            cols = slice(h * half_width, (h + 1) * half_width)
            grad_input = g_in[h].reshape(tokens, half_width).astype(F32) + scale_back * (
                accum[:, cols] * gain[:, cols] - mean_one - normed[:, cols] * mean_two
            )
            g_out[h] = grad_input.astype(BF16).reshape(batches, rows, half_width)
            backward_copies[h].start()

    finish_gather(fg)
    take_turn()
    far_part(fg, 0)
    near_part(fg, 0, 0)
    near_part(fg, 0, 1)
    far_part(fg, 1)
    relay_part(fg, 0)
    near_part(fg, 1, 0)
    near_part(fg, 1, 1)
    own_part(fg, 0)
    relay_part(fg, 1)
    own_part(fg, 1)
    collect(fg, 0)

    @pl.when(sec >= sections // 2)
    def _():
        act_products()
        collect(fa, 0)

    collect(fg, 1)
    finish(fa, 0, act_ref)
    finish(fg, 0, grad_ref)
    finish(fg, 1, grad_ref)

    @pl.when(sec < sections - 1)
    def _():
        for copy in forward_copies:
            copy.wait_send()

    @pl.when(sec > 0)
    def _():
        for copy in backward_copies:
            copy.wait_send()

    for f in (fa, fg):
        for copy in f.gathers:
            copy.wait_send()
        for g in range(f.groups):
            for d in range(2):
                f.far_copy[g][d].wait_send()
                for h in range(2):
                    f.near_copy[g][d][h].wait_send()
            for copy in f.z_copy[g]:
                copy.wait_send()


def scale_kernel(factor, act_ref, grad_ref, act_out, grad_out):
    act_out[0] = act_ref[...] * factor
    grad_out[0] = grad_ref[...] * factor


def body(dp_count, sections, inputs, ln_gain, w_in, w_out, layer_scale, out_grad, owner_table):
    batches, rows, width = inputs.shape
    hidden_width = w_in.shape[2]
    planes = dp_count // (RING * RING)
    block_a = width // dp_count
    block_g = hidden_width // dp_count
    tokens = batches * rows
    chunk = min(256, hidden_width // HALVES)
    dma = pltpu.SemaphoreType.DMA
    vmem = pl.BlockSpec(memory_space=pltpu.VMEM)
    hbm = pl.BlockSpec(memory_space=pl.ANY)

    def factor_scratch(block, extent, groups):
        span = planes * block
        half = extent // groups // 2
        others = max(planes - 1, 1)
        return [
            pltpu.VMEM((RING * span, extent), BF16),
            pltpu.VMEM((HALVES, RING, tokens, extent // HALVES), BF16),
            pltpu.VMEM((RING * span, RING * tokens), BF16),
            pltpu.VMEM((groups, 2, span, half), BF16),
            pltpu.VMEM((groups, 2, 2, span, half), BF16),
            pltpu.VMEM((groups, 2, span, half), F32),
            pltpu.VMEM((groups, span, 2 * half), F32),
            pltpu.VMEM((groups, 2, span, half), BF16),
            pltpu.VMEM((groups, 2, 2, span, half), BF16),
            pltpu.VMEM((groups, others, block, 2 * half), BF16),
            pltpu.VMEM((groups, others, block, 2 * half), BF16),
        ]

    act, grad = pl.pallas_call(
        functools.partial(kernel, dp_count, sections),
        out_shape=(
            jax.ShapeDtypeStruct((block_a, width), F32),
            jax.ShapeDtypeStruct((block_g, hidden_width), F32),
        ),
        in_specs=[pl.BlockSpec(memory_space=pltpu.SMEM), hbm, hbm, vmem, vmem, hbm, hbm],
        out_specs=(vmem, vmem),
        scratch_shapes=[
            pltpu.VMEM((width, hidden_width), BF16),
            pltpu.VMEM((hidden_width, width), BF16),
            pltpu.VMEM((HALVES, batches, rows, width // HALVES), BF16),
            pltpu.VMEM((HALVES, batches, rows, width // HALVES), BF16),
            pltpu.VMEM((HALVES, batches, rows, width // HALVES), BF16),
            pltpu.VMEM((HALVES, batches, rows, width // HALVES), BF16),
            pltpu.VMEM((tokens, width), F32),
            pltpu.VMEM((tokens, 1), F32),
            pltpu.VMEM((tokens, hidden_width), F32),
            pltpu.VMEM((tokens, width), F32),
            pltpu.VMEM((tokens, hidden_width), BF16),
            pltpu.VMEM((hidden_width, width), BF16),
            pltpu.VMEM((width, hidden_width), BF16),
        ]
        + factor_scratch(block_a, width, 1)
        + factor_scratch(block_g, hidden_width, 2)
        + [
            dma((2, hidden_width // chunk)),
            dma((2, HALVES * batches)),
            dma((2 * HALVES,)),
            dma((2 * HALVES,)),
            dma((2, 8)),
            dma((2, 8)),
            dma((2, 2, 6)),
            dma((2, 2, 6)),
            dma((2, 2, max(planes - 1, 1))),
            dma((2, 2, max(planes - 1, 1))),
            pltpu.SemaphoreType.REGULAR,
        ],
        compiler_params=pltpu.CompilerParams(
            collective_id=0, has_side_effects=True, vmem_limit_bytes=60 * 1024 * 1024
        ),
        name="window",
    )(owner_table, inputs, out_grad, ln_gain, layer_scale, w_in[0], w_out[0])
    factor = 1.0 / (tokens * dp_count)
    return pl.pallas_call(
        functools.partial(scale_kernel, factor),
        out_shape=(
            jax.ShapeDtypeStruct((1, block_a, width), F32),
            jax.ShapeDtypeStruct((1, block_g, hidden_width), F32),
        ),
        in_specs=[vmem, vmem],
        out_specs=(vmem, vmem),
        compiler_params=pltpu.CompilerParams(vmem_limit_bytes=60 * 1024 * 1024),
        name="mean",
    )(act, grad)


def solution(mesh):
    placed = (
        P(None, "dp", None),
        P("section", None),
        P("section", None, None),
        P("section", None, None),
        P("section", None),
        P(None, "dp", None),
        P(),
    )
    return jax.shard_map(
        functools.partial(body, mesh.shape["dp"], mesh.shape["section"]),
        mesh=mesh,
        in_specs=placed,
        out_specs=(P("section", "dp", None), P("section", "dp", None)),
        check_vma=False,
    )
```

```python
import functools
import jax
import jax.numpy as jnp
from jax import lax
from jax.experimental import pallas as pl
from jax.experimental.pallas import tpu as pltpu
from jax.sharding import PartitionSpec as P

SQRT_HALF = 0.7071067811865476
INV_ROOT_TAU = 0.3989422804014327
MESH = pl.DeviceIdType.MESH
F32 = jnp.float32
BF16 = jnp.bfloat16
NT = (((1,), (1,)), ((), ()))


RING = 4
HALVES = 2


def kernel(
    dp_count,
    sections,
    owner_ref,
    x_hbm,
    top_hbm,
    gain_ref,
    scale_ref,
    win_hbm,
    wout_hbm,
    act_ref,
    grad_ref,
    win,
    wout,
    x_in,
    y_out,
    g_in,
    g_out,
    normed,
    inv_std,
    slope,
    accum,
    acted,
    win_t,
    wout_t,
    *rest,
):
    (pick_a, rows_a, left_a, far_a, near_a, hold_a, sum_a, far_in_a, near_in_a, zs_a, zr_a) = rest[:11]
    (pick_g, rows_g, left_g, far_g, near_g, hold_g, sum_g, far_in_g, near_in_g, zs_g, zr_g) = rest[11:22]
    (w_sem, io_sem, relay_s, relay_r, gat_s, gat_r, sca_s, sca_r, z_s, z_r, turn) = rest[22:]
    planes = dp_count // (RING * RING)
    sec = lax.axis_index("section")
    me = lax.axis_index("dp")
    cx = me // (planes * RING)
    cz = lax.rem(me // RING, planes)
    cy = lax.rem(me, RING)
    even = lax.rem(sec, 2) == 0
    _, batches, rows, half_width = x_in.shape
    width = HALVES * half_width
    tokens = batches * rows
    hidden_width = win.shape[1]
    block_a = width // dp_count
    block_g = hidden_width // dp_count
    chunk = min(256, hidden_width // HALVES)
    chunks = hidden_width // chunk

    def index_of(px, pz, py):
        return px * planes * RING + pz * RING + py

    p = jnp.where(even, cx, cy)
    q = jnp.where(even, cy, cx)

    def at_pq(pp, pz, qq):
        return index_of(jnp.where(even, pp, qq), pz, jnp.where(even, qq, pp))

    def ring(value, k):
        return lax.rem(value + k + RING, RING)

    def p_peer(k):
        return (at_pq(ring(p, k), cz, q), sec)

    def q_peer(k):
        return (at_pq(p, cz, ring(q, k)), sec)

    def z_peer(k):
        return (index_of(cx, lax.rem(cz + k, planes), cy), sec)

    def remote(src, dst, ssem, rsem, device):
        return pltpu.make_async_remote_copy(
            src_ref=src, dst_ref=dst, send_sem=ssem, recv_sem=rsem,
            device_id=device, device_id_type=MESH,
        )

    load_in = []
    load_out = []
    for j in range(chunks):
        cols = pl.ds(j * chunk, chunk)
        load_in.append(pltpu.make_async_copy(win_hbm.at[:, cols], win.at[:, cols], w_sem.at[0, j]))
        load_out.append(pltpu.make_async_copy(wout_hbm.at[cols, :], wout.at[cols, :], w_sem.at[1, j]))
    load_x = []
    load_top = []
    for h in range(HALVES):
        cols = pl.ds(h * half_width, half_width)
        for m in range(batches):
            load_x.append(
                pltpu.make_async_copy(x_hbm.at[m, :, cols], x_in.at[h, m], io_sem.at[0, h * batches + m])
            )
            load_top.append(
                pltpu.make_async_copy(top_hbm.at[m, :, cols], g_in.at[h, m], io_sem.at[1, h * batches + m])
            )

    @pl.when(sec == 0)
    def _():
        for copy in load_x:
            copy.start()

    for copy in load_in:
        copy.start()
    for copy in load_out:
        copy.start()

    @pl.when(sec == sections - 1)
    def _():
        for copy in load_top:
            copy.start()

    barrier = pltpu.get_barrier_semaphore()
    greeted = [p_peer(1), p_peer(-1), q_peer(1), q_peer(-1)]
    greeted += [z_peer(k) for k in range(1, planes)]
    greeted += [(me, lax.rem(sec + 1, sections)), (me, lax.rem(sec + sections - 1, sections))]
    for device in greeted:
        pl.semaphore_signal(barrier, inc=1, device_id=device, device_id_type=MESH)

    def build_picks():
        for pick, block in ((pick_a, block_a), (pick_g, block_g)):
            extent = pick.shape[1]
            offset = lax.broadcasted_iota(jnp.int32, (block, extent), 1) - lax.broadcasted_iota(
                jnp.int32, (block, extent), 0
            )
            for qq in range(RING):
                for zz in range(planes):
                    owner = owner_ref[at_pq(p, zz, qq)]
                    row = (qq * planes + zz) * block
                    pick[row : row + block, :] = jnp.where(offset == owner * block, 1.0, 0.0).astype(BF16)

    forward_copies = [
        remote(y_out.at[h], x_in.at[h], relay_s.at[h], relay_r.at[h], (me, lax.rem(sec + 1, sections)))
        for h in range(HALVES)
    ]
    backward_copies = [
        remote(
            g_out.at[h], g_in.at[h], relay_s.at[HALVES + h], relay_r.at[HALVES + h],
            (me, lax.rem(sec + sections - 1, sections)),
        )
        for h in range(HALVES)
    ]

    class Factor:
        pass

    def factor(number, block, groups, pick, buffers):
        f = Factor()
        f.block, f.span, f.groups, f.pick = block, planes * block, groups, pick
        (f.rows, f.left, f.far, f.near, f.hold, f.total, f.far_in, f.near_in, f.zs, f.zr) = buffers
        f.half = f.far.shape[3]
        gs, gr = gat_s.at[number], gat_r.at[number]

        def row_copy(slot, h, part, n, k):
            piece = f.rows.at[h, slot]
            if part is not None:
                piece = f.rows.at[h, slot, pl.ds(part * (tokens // 2), tokens // 2)]
            return remote(piece, piece, gs.at[n], gr.at[n], p_peer(k))

        before, after = ring(p, -1), ring(p, 1)
        f.plus = [row_copy(p, 0, None, 0, 1), row_copy(p, 1, None, 1, 1), row_copy(before, 0, None, 2, 1)]
        f.minus = [row_copy(p, 0, None, 3, -1)]
        f.minus += [row_copy(p, 1, i, 4 + i, -1) for i in range(2)]
        f.minus += [row_copy(after, 1, i, 6 + i, -1) for i in range(2)]
        f.gathers = f.plus + f.minus
        ss, sr = sca_s.at[number], sca_r.at[number]
        f.far_copy = [
            [
                remote(f.far.at[g, d], f.far_in.at[g, d], ss.at[g, d], sr.at[g, d], q_peer((1, -1)[d]))
                for d in range(2)
            ]
            for g in range(groups)
        ]
        f.near_copy = [
            [
                [
                    remote(
                        f.near.at[g, d, h], f.near_in.at[g, d, h], ss.at[g, 2 + 2 * d + h],
                        sr.at[g, 2 + 2 * d + h], q_peer((1, -1)[d]),
                    )
                    for h in range(2)
                ]
                for d in range(2)
            ]
            for g in range(groups)
        ]
        f.z_copy = [
            [
                remote(
                    f.zs.at[g, k - 1], f.zr.at[g, k - 1], z_s.at[number, g, k - 1],
                    z_r.at[number, g, k - 1], z_peer(k),
                )
                for k in range(1, planes)
            ]
            for g in range(groups)
        ]
        return f

    fa = factor(0, block_a, 1, pick_a, (rows_a, left_a, far_a, near_a, hold_a, sum_a, far_in_a, near_in_a, zs_a, zr_a))
    fg = factor(1, block_g, 2, pick_g, (rows_g, left_g, far_g, near_g, hold_g, sum_g, far_in_g, near_in_g, zs_g, zr_g))

    def start_half(f, h):
        f.plus[h].start()
        if h == 0:
            f.minus[0].start()
        else:
            f.minus[1].start()
            f.minus[2].start()

    def choose(f, sources):
        extent = f.rows.shape[3]
        picked = None
        for h in range(HALVES):
            pieces = [f.rows[h, source] for source in sources]
            piece = pieces[0] if len(pieces) == 1 else jnp.concatenate(pieces, axis=0)
            part = lax.dot_general(
                f.pick[:, h * extent : (h + 1) * extent], piece, NT, preferred_element_type=F32
            )
            picked = part if picked is None else picked + part
        for i, source in enumerate(sources):
            f.left[:, pl.ds(pl.multiple_of(source * tokens, tokens), tokens)] = picked[
                :, i * tokens : (i + 1) * tokens
            ].astype(BF16)

    def give_turn():
        @pl.when(even)
        def _():
            pl.semaphore_signal(turn, inc=1, device_id=(me, lax.rem(sec + 1, sections)), device_id_type=MESH)

    def take_turn():
        @pl.when(jnp.logical_not(even))
        def _():
            pl.semaphore_wait(turn, 1)

    def finish_gather(f):
        choose(f, [p])
        f.plus[0].wait_recv()
        f.plus[2].start()
        f.minus[1].wait_recv()
        f.minus[3].start()
        f.minus[2].wait_recv()
        f.minus[4].start()
        f.plus[1].wait_recv()
        f.minus[0].wait_recv()
        if f is fg:
            give_turn()
        choose(f, [ring(p, -1), ring(p, 1)])
        f.plus[2].wait_recv()
        f.minus[3].wait_recv()
        f.minus[4].wait_recv()
        choose(f, [ring(p, 2)])

    def part_of(f, g, k):
        extent = f.rows.shape[3]
        dest = ring(q, k)
        left = f.left[pl.ds(pl.multiple_of(dest * f.span, f.span), f.span), :]
        pieces = [
            jnp.dot(left, f.rows[h].reshape(RING * tokens, extent), preferred_element_type=F32)
            for h in ((g,) if f.groups == 2 else range(HALVES))
        ]
        return pieces[0] if len(pieces) == 1 else jnp.concatenate(pieces, axis=1)

    def far_part(f, g):
        part = part_of(f, g, 2)
        for d in range(2):
            f.far[g, d] = part[:, d * f.half : (d + 1) * f.half].astype(BF16)
            f.far_copy[g][d].start()

    def near_part(f, g, d):
        part = part_of(f, g, (1, -1)[d])
        free = 1 - d
        f.near[g, d, free] = part[:, free * f.half : (free + 1) * f.half].astype(BF16)
        f.near_copy[g][d][free].start()
        f.hold[g, d] = part[:, d * f.half : (d + 1) * f.half]

    def own_part(f, g):
        f.total[g] = part_of(f, g, 0)

    def relay_part(f, g):
        for d in range(2):
            f.far_copy[g][d].wait_recv()
            f.near[g, d, d] = (f.hold[g, d] + f.far_in[g, d].astype(F32)).astype(BF16)
            f.near_copy[g][d][d].start()

    def collect(f, g):
        for d in range(2):
            for h in range(2):
                f.near_copy[g][d][h].wait_recv()
        for h in range(2):
            cols = slice(h * f.half, (h + 1) * f.half)
            f.total[g, :, cols] += f.near_in[g, 0, h].astype(F32) + f.near_in[g, 1, h].astype(F32)
        for k in range(1, planes):
            dest = lax.rem(cz + k, planes)
            f.zs[g, k - 1] = f.total[g, pl.ds(pl.multiple_of(dest * f.block, f.block), f.block), :].astype(BF16)
            f.z_copy[g][k - 1].start()

    def finish(f, g, out):
        for copy in f.z_copy[g]:
            copy.wait_recv()
        value = f.total[g, pl.ds(pl.multiple_of(cz * f.block, f.block), f.block), :]
        for k in range(1, planes):
            value = value + f.zr[g, k - 1].astype(F32)
        out[:, g * 2 * f.half : (g + 1) * 2 * f.half] = value

    def act_products():
        finish_gather(fa)
        far_part(fa, 0)
        near_part(fa, 0, 0)
        near_part(fa, 0, 1)
        own_part(fa, 0)
        relay_part(fa, 0)

    def transpose_weights():
        for source, target in ((wout, wout_t), (win, win_t)):
            count = source.shape[0] // chunk

            def step(i, carry):
                at = pl.ds(pl.multiple_of(i * chunk, chunk), chunk)
                target[:, at] = source[at, :].T
                return carry

            lax.fori_loop(0, count, step, 0)

    gain = gain_ref[...]
    scales = scale_ref[...]

    @pl.when(sec > 0)
    def _():
        build_picks()
        for copy in load_in + load_out:
            copy.wait()

        @pl.when(sec == sections - 1)
        def _():
            transpose_weights()

        for copy in forward_copies:
            copy.wait_recv()

    @pl.when(sec == 0)
    def _():
        for copy in load_x:
            copy.wait()

    def joined(ref):
        return jnp.concatenate([ref[h].reshape(tokens, half_width) for h in range(HALVES)], axis=1)

    floats = joined(x_in).astype(F32)
    center = floats - jnp.mean(floats, axis=-1, keepdims=True)
    inverse = lax.rsqrt(jnp.mean(center * center, axis=-1, keepdims=True) + 1e-06)
    normal = center * inverse
    normed[...] = normal
    inv_std[...] = inverse
    scaled_rows = (normal * gain).astype(BF16)
    for h in range(HALVES):
        rows_a[h, p] = scaled_rows[:, h * half_width : (h + 1) * half_width]

    def forward_chunk(j, scaled):
        cols = slice(j * chunk, (j + 1) * chunk)
        hidden = jnp.dot(scaled, win[:, cols], preferred_element_type=F32)
        cdf = 0.5 * (1.0 + lax.erf(hidden * SQRT_HALF))
        acted[:, cols] = (hidden * cdf).astype(BF16)
        slope[:, cols] = cdf + hidden * INV_ROOT_TAU * jnp.exp(-0.5 * hidden * hidden)

    @pl.when(sec == 0)
    def _():
        for copy in load_in:
            copy.wait()

    scaled = jnp.concatenate([rows_a[h, p] for h in range(HALVES)], axis=1)
    for j in range(chunks):
        forward_chunk(j, scaled)

    @pl.when(sec == 0)
    def _():
        for copy in load_out:
            copy.wait()

    pl.semaphore_wait(barrier, len(greeted))

    @pl.when(sec < sections - 1)
    def _():
        values = acted[...]
        for h in range(HALVES):
            cols = slice(h * half_width, (h + 1) * half_width)
            part = jnp.dot(values, wout[:, cols], preferred_element_type=F32)
            output = x_in[h].reshape(tokens, half_width).astype(F32) + scales[:, cols] * part
            y_out[h] = output.astype(BF16).reshape(batches, rows, half_width)
            forward_copies[h].start()

    for h in range(HALVES):
        start_half(fa, h)

    @pl.when(sec == 0)
    def _():
        build_picks()

    @pl.when(sec < sections - 1)
    def _():
        transpose_weights()

    @pl.when(sec < sections // 2)
    def _():
        act_products()
        collect(fa, 0)

    @pl.when(sec < sections - 1)
    def _():
        for copy in backward_copies:
            copy.wait_recv()

    @pl.when(sec == sections - 1)
    def _():
        for copy in load_top:
            copy.wait()

    cotangent = joined(g_in).astype(F32)
    gz = (cotangent * scales).astype(BF16)
    per = chunks // HALVES
    for j in range(chunks):
        cols = slice(j * chunk, (j + 1) * chunk)
        grad_act = jnp.dot(gz, wout_t[:, cols], preferred_element_type=F32)
        h, inner = j // per, j % per
        rows_g[h, p, :, inner * chunk : (inner + 1) * chunk] = (grad_act * slope[:, cols]).astype(BF16)
        if inner == per - 1:
            start_half(fg, h)

    @pl.when(sec > 0)
    def _():
        grad_hidden = jnp.concatenate([rows_g[h, p] for h in range(HALVES)], axis=1)
        sum_one = sum_two = None
        for n in range(width // chunk):
            cols = slice(n * chunk, (n + 1) * chunk)
            piece = jnp.dot(grad_hidden, win_t[:, cols], preferred_element_type=F32) * gain[:, cols]
            accum[:, cols] = piece
            one = jnp.sum(piece, axis=-1, keepdims=True)
            two = jnp.sum(piece * normed[:, cols], axis=-1, keepdims=True)
            sum_one = one if n == 0 else sum_one + one
            sum_two = two if n == 0 else sum_two + two
        mean_one = sum_one / width
        mean_two = sum_two / width
        scale_back = inv_std[...]
        for h in range(HALVES):
            cols = slice(h * half_width, (h + 1) * half_width)
            grad_input = g_in[h].reshape(tokens, half_width).astype(F32) + scale_back * (
                accum[:, cols] - mean_one - normed[:, cols] * mean_two
            )
            g_out[h] = grad_input.astype(BF16).reshape(batches, rows, half_width)
            backward_copies[h].start()

    finish_gather(fg)
    take_turn()
    far_part(fg, 0)
    near_part(fg, 0, 0)
    near_part(fg, 0, 1)
    far_part(fg, 1)
    relay_part(fg, 0)
    near_part(fg, 1, 0)
    near_part(fg, 1, 1)
    own_part(fg, 0)
    relay_part(fg, 1)
    own_part(fg, 1)
    collect(fg, 0)

    @pl.when(sec >= sections // 2)
    def _():
        act_products()
        collect(fa, 0)

    collect(fg, 1)
    finish(fa, 0, act_ref)
    finish(fg, 0, grad_ref)
    finish(fg, 1, grad_ref)

    @pl.when(sec < sections - 1)
    def _():
        for copy in forward_copies:
            copy.wait_send()

    @pl.when(sec > 0)
    def _():
        for copy in backward_copies:
            copy.wait_send()

    for f in (fa, fg):
        for copy in f.gathers:
            copy.wait_send()
        for g in range(f.groups):
            for d in range(2):
                f.far_copy[g][d].wait_send()
                for h in range(2):
                    f.near_copy[g][d][h].wait_send()
            for copy in f.z_copy[g]:
                copy.wait_send()


def scale_kernel(factor, act_ref, grad_ref, act_out, grad_out):
    act_out[0] = act_ref[...] * factor
    grad_out[0] = grad_ref[...] * factor


def body(dp_count, sections, inputs, ln_gain, w_in, w_out, layer_scale, out_grad, owner_table):
    batches, rows, width = inputs.shape
    hidden_width = w_in.shape[2]
    planes = dp_count // (RING * RING)
    block_a = width // dp_count
    block_g = hidden_width // dp_count
    tokens = batches * rows
    chunk = min(256, hidden_width // HALVES)
    dma = pltpu.SemaphoreType.DMA
    vmem = pl.BlockSpec(memory_space=pltpu.VMEM)
    hbm = pl.BlockSpec(memory_space=pl.ANY)

    def factor_scratch(block, extent, groups):
        span = planes * block
        half = extent // groups // 2
        others = max(planes - 1, 1)
        return [
            pltpu.VMEM((RING * span, extent), BF16),
            pltpu.VMEM((HALVES, RING, tokens, extent // HALVES), BF16),
            pltpu.VMEM((RING * span, RING * tokens), BF16),
            pltpu.VMEM((groups, 2, span, half), BF16),
            pltpu.VMEM((groups, 2, 2, span, half), BF16),
            pltpu.VMEM((groups, 2, span, half), F32),
            pltpu.VMEM((groups, span, 2 * half), F32),
            pltpu.VMEM((groups, 2, span, half), BF16),
            pltpu.VMEM((groups, 2, 2, span, half), BF16),
            pltpu.VMEM((groups, others, block, 2 * half), BF16),
            pltpu.VMEM((groups, others, block, 2 * half), BF16),
        ]

    act, grad = pl.pallas_call(
        functools.partial(kernel, dp_count, sections),
        out_shape=(
            jax.ShapeDtypeStruct((block_a, width), F32),
            jax.ShapeDtypeStruct((block_g, hidden_width), F32),
        ),
        in_specs=[pl.BlockSpec(memory_space=pltpu.SMEM), hbm, hbm, vmem, vmem, hbm, hbm],
        out_specs=(vmem, vmem),
        scratch_shapes=[
            pltpu.VMEM((width, hidden_width), BF16),
            pltpu.VMEM((hidden_width, width), BF16),
            pltpu.VMEM((HALVES, batches, rows, width // HALVES), BF16),
            pltpu.VMEM((HALVES, batches, rows, width // HALVES), BF16),
            pltpu.VMEM((HALVES, batches, rows, width // HALVES), BF16),
            pltpu.VMEM((HALVES, batches, rows, width // HALVES), BF16),
            pltpu.VMEM((tokens, width), F32),
            pltpu.VMEM((tokens, 1), F32),
            pltpu.VMEM((tokens, hidden_width), F32),
            pltpu.VMEM((tokens, width), F32),
            pltpu.VMEM((tokens, hidden_width), BF16),
            pltpu.VMEM((hidden_width, width), BF16),
            pltpu.VMEM((width, hidden_width), BF16),
        ]
        + factor_scratch(block_a, width, 1)
        + factor_scratch(block_g, hidden_width, 2)
        + [
            dma((2, hidden_width // chunk)),
            dma((2, HALVES * batches)),
            dma((2 * HALVES,)),
            dma((2 * HALVES,)),
            dma((2, 8)),
            dma((2, 8)),
            dma((2, 2, 6)),
            dma((2, 2, 6)),
            dma((2, 2, max(planes - 1, 1))),
            dma((2, 2, max(planes - 1, 1))),
            pltpu.SemaphoreType.REGULAR,
        ],
        compiler_params=pltpu.CompilerParams(
            collective_id=0, has_side_effects=True, vmem_limit_bytes=60 * 1024 * 1024
        ),
        name="window",
    )(owner_table, inputs, out_grad, ln_gain, layer_scale, w_in[0], w_out[0])
    factor = 1.0 / (tokens * dp_count)
    return pl.pallas_call(
        functools.partial(scale_kernel, factor),
        out_shape=(
            jax.ShapeDtypeStruct((1, block_a, width), F32),
            jax.ShapeDtypeStruct((1, block_g, hidden_width), F32),
        ),
        in_specs=[vmem, vmem],
        out_specs=(vmem, vmem),
        compiler_params=pltpu.CompilerParams(vmem_limit_bytes=60 * 1024 * 1024),
        name="mean",
    )(act, grad)


def solution(mesh):
    placed = (
        P(None, "dp", None),
        P("section", None),
        P("section", None, None),
        P("section", None, None),
        P("section", None),
        P(None, "dp", None),
        P(),
    )
    return jax.shard_map(
        functools.partial(body, mesh.shape["dp"], mesh.shape["section"]),
        mesh=mesh,
        in_specs=placed,
        out_specs=(P("section", "dp", None), P("section", "dp", None)),
        check_vma=False,
    )
```

```python
import functools
import jax
import jax.numpy as jnp
from jax import lax
from jax.experimental import pallas as pl
from jax.experimental.pallas import tpu as pltpu
from jax.sharding import PartitionSpec as P

SQRT_HALF = 0.7071067811865476
INV_ROOT_TAU = 0.3989422804014327
MESH = pl.DeviceIdType.MESH
F32 = jnp.float32
BF16 = jnp.bfloat16
NT = (((1,), (1,)), ((), ()))


RING = 4
HALVES = 2


def kernel(
    dp_count,
    sections,
    owner_ref,
    x_hbm,
    top_hbm,
    gain_ref,
    scale_ref,
    win_hbm,
    wout_hbm,
    act_ref,
    grad_ref,
    win,
    wout,
    x_in,
    y_out,
    g_in,
    g_out,
    normed,
    inv_std,
    slope,
    accum,
    acted,
    win_t,
    wout_t,
    *rest,
):
    (pick_a, rows_a, left_a, far_a, near_a, hold_a, sum_a, far_in_a, near_in_a, zs_a, zr_a) = rest[:11]
    (pick_g, rows_g, left_g, far_g, near_g, hold_g, sum_g, far_in_g, near_in_g, zs_g, zr_g) = rest[11:22]
    (w_sem, io_sem, relay_s, relay_r, gat_s, gat_r, sca_s, sca_r, z_s, z_r, turn) = rest[22:]
    planes = dp_count // (RING * RING)
    sec = lax.axis_index("section")
    me = lax.axis_index("dp")
    cx = me // (planes * RING)
    cz = lax.rem(me // RING, planes)
    cy = lax.rem(me, RING)
    even = lax.rem(sec, 2) == 0
    _, batches, rows, half_width = x_in.shape
    width = HALVES * half_width
    tokens = batches * rows
    hidden_width = win.shape[1]
    block_a = width // dp_count
    block_g = hidden_width // dp_count
    chunk = min(256, hidden_width // HALVES)
    chunks = hidden_width // chunk

    def index_of(px, pz, py):
        return px * planes * RING + pz * RING + py

    p = jnp.where(even, cx, cy)
    q = jnp.where(even, cy, cx)

    def at_pq(pp, pz, qq):
        return index_of(jnp.where(even, pp, qq), pz, jnp.where(even, qq, pp))

    def ring(value, k):
        return lax.rem(value + k + RING, RING)

    def p_peer(k):
        return (at_pq(ring(p, k), cz, q), sec)

    def q_peer(k):
        return (at_pq(p, cz, ring(q, k)), sec)

    def z_peer(k):
        return (index_of(cx, lax.rem(cz + k, planes), cy), sec)

    def remote(src, dst, ssem, rsem, device):
        return pltpu.make_async_remote_copy(
            src_ref=src, dst_ref=dst, send_sem=ssem, recv_sem=rsem,
            device_id=device, device_id_type=MESH,
        )

    load_in = []
    load_out = []
    for j in range(chunks):
        cols = pl.ds(j * chunk, chunk)
        load_in.append(pltpu.make_async_copy(win_hbm.at[:, cols], win.at[:, cols], w_sem.at[0, j]))
        load_out.append(pltpu.make_async_copy(wout_hbm.at[cols, :], wout.at[cols, :], w_sem.at[1, j]))
    load_x = []
    load_top = []
    for h in range(HALVES):
        cols = pl.ds(h * half_width, half_width)
        for m in range(batches):
            load_x.append(
                pltpu.make_async_copy(x_hbm.at[m, :, cols], x_in.at[h, m], io_sem.at[0, h * batches + m])
            )
            load_top.append(
                pltpu.make_async_copy(top_hbm.at[m, :, cols], g_in.at[h, m], io_sem.at[1, h * batches + m])
            )

    @pl.when(sec == 0)
    def _():
        for copy in load_x:
            copy.start()

    for copy in load_in:
        copy.start()
    for copy in load_out:
        copy.start()

    @pl.when(sec == sections - 1)
    def _():
        for copy in load_top:
            copy.start()

    barrier = pltpu.get_barrier_semaphore()
    greeted = [p_peer(1), p_peer(-1), q_peer(1), q_peer(-1)]
    greeted += [z_peer(k) for k in range(1, planes)]
    greeted += [(me, lax.rem(sec + 1, sections)), (me, lax.rem(sec + sections - 1, sections))]
    for device in greeted:
        pl.semaphore_signal(barrier, inc=1, device_id=device, device_id_type=MESH)

    def build_picks():
        for pick, block in ((pick_a, block_a), (pick_g, block_g)):
            extent = pick.shape[1]
            offset = lax.broadcasted_iota(jnp.int32, (block, extent), 1) - lax.broadcasted_iota(
                jnp.int32, (block, extent), 0
            )
            for qq in range(RING):
                for zz in range(planes):
                    owner = owner_ref[at_pq(p, zz, qq)]
                    row = (qq * planes + zz) * block
                    pick[row : row + block, :] = jnp.where(offset == owner * block, 1.0, 0.0).astype(BF16)

    forward_copies = [
        remote(y_out.at[h], x_in.at[h], relay_s.at[h], relay_r.at[h], (me, lax.rem(sec + 1, sections)))
        for h in range(HALVES)
    ]
    backward_copies = [
        remote(
            g_out.at[h], g_in.at[h], relay_s.at[HALVES + h], relay_r.at[HALVES + h],
            (me, lax.rem(sec + sections - 1, sections)),
        )
        for h in range(HALVES)
    ]

    class Factor:
        pass

    def factor(number, block, groups, pick, buffers):
        f = Factor()
        f.block, f.span, f.groups, f.pick = block, planes * block, groups, pick
        (f.rows, f.left, f.far, f.near, f.hold, f.total, f.far_in, f.near_in, f.zs, f.zr) = buffers
        f.half = f.far.shape[3]
        gs, gr = gat_s.at[number], gat_r.at[number]

        def row_copy(slot, h, part, n, k):
            piece = f.rows.at[h, slot]
            if part is not None:
                piece = f.rows.at[h, slot, pl.ds(part * (tokens // 2), tokens // 2)]
            return remote(piece, piece, gs.at[n], gr.at[n], p_peer(k))

        before, after = ring(p, -1), ring(p, 1)
        f.plus = [row_copy(p, 0, None, 0, 1), row_copy(p, 1, None, 1, 1), row_copy(before, 0, None, 2, 1)]
        f.minus = [row_copy(p, 0, None, 3, -1)]
        f.minus += [row_copy(p, 1, i, 4 + i, -1) for i in range(2)]
        f.minus += [row_copy(after, 1, i, 6 + i, -1) for i in range(2)]
        f.gathers = f.plus + f.minus
        ss, sr = sca_s.at[number], sca_r.at[number]
        f.far_copy = [
            [
                remote(f.far.at[g, d], f.far_in.at[g, d], ss.at[g, d], sr.at[g, d], q_peer((1, -1)[d]))
                for d in range(2)
            ]
            for g in range(groups)
        ]
        f.near_copy = [
            [
                [
                    remote(
                        f.near.at[g, d, h], f.near_in.at[g, d, h], ss.at[g, 2 + 2 * d + h],
                        sr.at[g, 2 + 2 * d + h], q_peer((1, -1)[d]),
                    )
                    for h in range(2)
                ]
                for d in range(2)
            ]
            for g in range(groups)
        ]
        f.z_copy = [
            [
                remote(
                    f.zs.at[g, k - 1], f.zr.at[g, k - 1], z_s.at[number, g, k - 1],
                    z_r.at[number, g, k - 1], z_peer(k),
                )
                for k in range(1, planes)
            ]
            for g in range(groups)
        ]
        return f

    fa = factor(0, block_a, 1, pick_a, (rows_a, left_a, far_a, near_a, hold_a, sum_a, far_in_a, near_in_a, zs_a, zr_a))
    fg = factor(1, block_g, 2, pick_g, (rows_g, left_g, far_g, near_g, hold_g, sum_g, far_in_g, near_in_g, zs_g, zr_g))

    def start_half(f, h):
        f.plus[h].start()
        if h == 0:
            f.minus[0].start()
        else:
            f.minus[1].start()
            f.minus[2].start()

    def choose(f, sources):
        extent = f.rows.shape[3]
        picked = None
        for h in range(HALVES):
            pieces = [f.rows[h, source] for source in sources]
            piece = pieces[0] if len(pieces) == 1 else jnp.concatenate(pieces, axis=0)
            part = lax.dot_general(
                f.pick[:, h * extent : (h + 1) * extent], piece, NT, preferred_element_type=F32
            )
            picked = part if picked is None else picked + part
        for i, source in enumerate(sources):
            f.left[:, pl.ds(pl.multiple_of(source * tokens, tokens), tokens)] = picked[
                :, i * tokens : (i + 1) * tokens
            ].astype(BF16)

    def give_turn():
        @pl.when(even)
        def _():
            pl.semaphore_signal(turn, inc=1, device_id=(me, lax.rem(sec + 1, sections)), device_id_type=MESH)

    def take_turn():
        @pl.when(jnp.logical_not(even))
        def _():
            pl.semaphore_wait(turn, 1)

    def finish_gather(f):
        choose(f, [p])
        f.plus[0].wait_recv()
        f.plus[2].start()
        f.minus[1].wait_recv()
        f.minus[3].start()
        f.minus[2].wait_recv()
        f.minus[4].start()
        f.plus[1].wait_recv()
        f.minus[0].wait_recv()
        if f is fg:
            give_turn()
        choose(f, [ring(p, -1), ring(p, 1)])
        f.plus[2].wait_recv()
        f.minus[3].wait_recv()
        f.minus[4].wait_recv()
        choose(f, [ring(p, 2)])

    def part_of(f, g, k):
        extent = f.rows.shape[3]
        dest = ring(q, k)
        left = f.left[pl.ds(pl.multiple_of(dest * f.span, f.span), f.span), :]
        pieces = [
            jnp.dot(left, f.rows[h].reshape(RING * tokens, extent), preferred_element_type=F32)
            for h in ((g,) if f.groups == 2 else range(HALVES))
        ]
        return pieces[0] if len(pieces) == 1 else jnp.concatenate(pieces, axis=1)

    def far_part(f, g):
        dest = ring(q, 2)
        extent = f.rows.shape[3]
        left = f.left[pl.ds(pl.multiple_of(dest * f.span, f.span), f.span), :]
        for d in range(2):
            at = g * 2 * f.half + d * f.half
            source = f.rows[at // extent, :, :, at % extent : at % extent + f.half]
            part = jnp.dot(left, source.reshape(RING * tokens, f.half), preferred_element_type=F32)
            f.far[g, d] = part.astype(BF16)
            f.far_copy[g][d].start()

    def near_part(f, g, d):
        part = part_of(f, g, (1, -1)[d])
        free = 1 - d
        f.near[g, d, free] = part[:, free * f.half : (free + 1) * f.half].astype(BF16)
        f.near_copy[g][d][free].start()
        f.hold[g, d] = part[:, d * f.half : (d + 1) * f.half]

    def own_part(f, g):
        f.total[g] = part_of(f, g, 0)

    def relay_part(f, g):
        for d in range(2):
            f.far_copy[g][d].wait_recv()
            f.near[g, d, d] = (f.hold[g, d] + f.far_in[g, d].astype(F32)).astype(BF16)
            f.near_copy[g][d][d].start()

    def collect(f, g):
        for d in range(2):
            for h in range(2):
                f.near_copy[g][d][h].wait_recv()
        for h in range(2):
            cols = slice(h * f.half, (h + 1) * f.half)
            f.total[g, :, cols] += f.near_in[g, 0, h].astype(F32) + f.near_in[g, 1, h].astype(F32)
        for k in range(1, planes):
            dest = lax.rem(cz + k, planes)
            f.zs[g, k - 1] = f.total[g, pl.ds(pl.multiple_of(dest * f.block, f.block), f.block), :].astype(BF16)
            f.z_copy[g][k - 1].start()

    def finish(f, g, out):
        for copy in f.z_copy[g]:
            copy.wait_recv()
        value = f.total[g, pl.ds(pl.multiple_of(cz * f.block, f.block), f.block), :]
        for k in range(1, planes):
            value = value + f.zr[g, k - 1].astype(F32)
        out[:, g * 2 * f.half : (g + 1) * 2 * f.half] = value

    def act_products():
        finish_gather(fa)
        far_part(fa, 0)
        near_part(fa, 0, 0)
        near_part(fa, 0, 1)
        own_part(fa, 0)
        relay_part(fa, 0)

    def transpose_weights():
        for source, target in ((wout, wout_t), (win, win_t)):
            count = source.shape[0] // chunk

            def step(i, carry):
                at = pl.ds(pl.multiple_of(i * chunk, chunk), chunk)
                target[:, at] = source[at, :].T
                return carry

            lax.fori_loop(0, count, step, 0)

    gain = gain_ref[...]
    scales = scale_ref[...]

    @pl.when(sec > 0)
    def _():
        build_picks()
        for copy in load_in + load_out:
            copy.wait()

        @pl.when(sec == sections - 1)
        def _():
            transpose_weights()

        for copy in forward_copies:
            copy.wait_recv()

    @pl.when(sec == 0)
    def _():
        for copy in load_x:
            copy.wait()

    def joined(ref):
        return jnp.concatenate([ref[h].reshape(tokens, half_width) for h in range(HALVES)], axis=1)

    floats = joined(x_in).astype(F32)
    center = floats - jnp.mean(floats, axis=-1, keepdims=True)
    inverse = lax.rsqrt(jnp.mean(center * center, axis=-1, keepdims=True) + 1e-06)
    normal = center * inverse
    normed[...] = normal
    inv_std[...] = inverse
    scaled_rows = (normal * gain).astype(BF16)
    for h in range(HALVES):
        rows_a[h, p] = scaled_rows[:, h * half_width : (h + 1) * half_width]

    def forward_chunk(j, scaled):
        cols = slice(j * chunk, (j + 1) * chunk)
        hidden = jnp.dot(scaled, win[:, cols], preferred_element_type=F32)
        cdf = 0.5 * (1.0 + lax.erf(hidden * SQRT_HALF))
        acted[:, cols] = (hidden * cdf).astype(BF16)
        slope[:, cols] = cdf + hidden * INV_ROOT_TAU * jnp.exp(-0.5 * hidden * hidden)

    @pl.when(sec == 0)
    def _():
        for copy in load_in:
            copy.wait()

    scaled = jnp.concatenate([rows_a[h, p] for h in range(HALVES)], axis=1)
    for j in range(chunks):
        forward_chunk(j, scaled)

    @pl.when(sec == 0)
    def _():
        for copy in load_out:
            copy.wait()

    pl.semaphore_wait(barrier, len(greeted))

    @pl.when(sec < sections - 1)
    def _():
        values = acted[...]
        for h in range(HALVES):
            cols = slice(h * half_width, (h + 1) * half_width)
            part = jnp.dot(values, wout[:, cols], preferred_element_type=F32)
            output = x_in[h].reshape(tokens, half_width).astype(F32) + scales[:, cols] * part
            y_out[h] = output.astype(BF16).reshape(batches, rows, half_width)
            forward_copies[h].start()

    for h in range(HALVES):
        start_half(fa, h)

    @pl.when(sec == 0)
    def _():
        build_picks()

    @pl.when(sec < sections - 1)
    def _():
        transpose_weights()

    @pl.when(sec < sections // 2)
    def _():
        act_products()
        collect(fa, 0)

    @pl.when(sec < sections - 1)
    def _():
        for copy in backward_copies:
            copy.wait_recv()

    @pl.when(sec == sections - 1)
    def _():
        for copy in load_top:
            copy.wait()

    cotangent = joined(g_in).astype(F32)
    gz = (cotangent * scales).astype(BF16)
    per = chunks // HALVES
    for j in range(chunks):
        cols = slice(j * chunk, (j + 1) * chunk)
        grad_act = jnp.dot(gz, wout_t[:, cols], preferred_element_type=F32)
        h, inner = j // per, j % per
        rows_g[h, p, :, inner * chunk : (inner + 1) * chunk] = (grad_act * slope[:, cols]).astype(BF16)
        if inner == per - 1:
            start_half(fg, h)

    @pl.when(sec > 0)
    def _():
        grad_hidden = jnp.concatenate([rows_g[h, p] for h in range(HALVES)], axis=1)
        sum_one = sum_two = None
        for n in range(width // chunk):
            cols = slice(n * chunk, (n + 1) * chunk)
            piece = jnp.dot(grad_hidden, win_t[:, cols], preferred_element_type=F32) * gain[:, cols]
            accum[:, cols] = piece
            one = jnp.sum(piece, axis=-1, keepdims=True)
            two = jnp.sum(piece * normed[:, cols], axis=-1, keepdims=True)
            sum_one = one if n == 0 else sum_one + one
            sum_two = two if n == 0 else sum_two + two
        mean_one = sum_one / width
        mean_two = sum_two / width
        scale_back = inv_std[...]
        for h in range(HALVES):
            cols = slice(h * half_width, (h + 1) * half_width)
            grad_input = g_in[h].reshape(tokens, half_width).astype(F32) + scale_back * (
                accum[:, cols] - mean_one - normed[:, cols] * mean_two
            )
            g_out[h] = grad_input.astype(BF16).reshape(batches, rows, half_width)
            backward_copies[h].start()

    finish_gather(fg)
    take_turn()
    far_part(fg, 0)
    near_part(fg, 0, 0)
    near_part(fg, 0, 1)
    far_part(fg, 1)
    relay_part(fg, 0)
    near_part(fg, 1, 0)
    near_part(fg, 1, 1)
    own_part(fg, 0)
    relay_part(fg, 1)
    own_part(fg, 1)
    collect(fg, 0)

    @pl.when(sec >= sections // 2)
    def _():
        act_products()
        collect(fa, 0)

    collect(fg, 1)
    finish(fa, 0, act_ref)
    finish(fg, 0, grad_ref)
    finish(fg, 1, grad_ref)

    @pl.when(sec < sections - 1)
    def _():
        for copy in forward_copies:
            copy.wait_send()

    @pl.when(sec > 0)
    def _():
        for copy in backward_copies:
            copy.wait_send()

    for f in (fa, fg):
        for copy in f.gathers:
            copy.wait_send()
        for g in range(f.groups):
            for d in range(2):
                f.far_copy[g][d].wait_send()
                for h in range(2):
                    f.near_copy[g][d][h].wait_send()
            for copy in f.z_copy[g]:
                copy.wait_send()


def scale_kernel(factor, act_ref, grad_ref, act_out, grad_out):
    act_out[0] = act_ref[...] * factor
    grad_out[0] = grad_ref[...] * factor


def body(dp_count, sections, inputs, ln_gain, w_in, w_out, layer_scale, out_grad, owner_table):
    batches, rows, width = inputs.shape
    hidden_width = w_in.shape[2]
    planes = dp_count // (RING * RING)
    block_a = width // dp_count
    block_g = hidden_width // dp_count
    tokens = batches * rows
    chunk = min(256, hidden_width // HALVES)
    dma = pltpu.SemaphoreType.DMA
    vmem = pl.BlockSpec(memory_space=pltpu.VMEM)
    hbm = pl.BlockSpec(memory_space=pl.ANY)

    def factor_scratch(block, extent, groups):
        span = planes * block
        half = extent // groups // 2
        others = max(planes - 1, 1)
        return [
            pltpu.VMEM((RING * span, extent), BF16),
            pltpu.VMEM((HALVES, RING, tokens, extent // HALVES), BF16),
            pltpu.VMEM((RING * span, RING * tokens), BF16),
            pltpu.VMEM((groups, 2, span, half), BF16),
            pltpu.VMEM((groups, 2, 2, span, half), BF16),
            pltpu.VMEM((groups, 2, span, half), F32),
            pltpu.VMEM((groups, span, 2 * half), F32),
            pltpu.VMEM((groups, 2, span, half), BF16),
            pltpu.VMEM((groups, 2, 2, span, half), BF16),
            pltpu.VMEM((groups, others, block, 2 * half), BF16),
            pltpu.VMEM((groups, others, block, 2 * half), BF16),
        ]

    act, grad = pl.pallas_call(
        functools.partial(kernel, dp_count, sections),
        out_shape=(
            jax.ShapeDtypeStruct((block_a, width), F32),
            jax.ShapeDtypeStruct((block_g, hidden_width), F32),
        ),
        in_specs=[pl.BlockSpec(memory_space=pltpu.SMEM), hbm, hbm, vmem, vmem, hbm, hbm],
        out_specs=(vmem, vmem),
        scratch_shapes=[
            pltpu.VMEM((width, hidden_width), BF16),
            pltpu.VMEM((hidden_width, width), BF16),
            pltpu.VMEM((HALVES, batches, rows, width // HALVES), BF16),
            pltpu.VMEM((HALVES, batches, rows, width // HALVES), BF16),
            pltpu.VMEM((HALVES, batches, rows, width // HALVES), BF16),
            pltpu.VMEM((HALVES, batches, rows, width // HALVES), BF16),
            pltpu.VMEM((tokens, width), F32),
            pltpu.VMEM((tokens, 1), F32),
            pltpu.VMEM((tokens, hidden_width), F32),
            pltpu.VMEM((tokens, width), F32),
            pltpu.VMEM((tokens, hidden_width), BF16),
            pltpu.VMEM((hidden_width, width), BF16),
            pltpu.VMEM((width, hidden_width), BF16),
        ]
        + factor_scratch(block_a, width, 1)
        + factor_scratch(block_g, hidden_width, 2)
        + [
            dma((2, hidden_width // chunk)),
            dma((2, HALVES * batches)),
            dma((2 * HALVES,)),
            dma((2 * HALVES,)),
            dma((2, 8)),
            dma((2, 8)),
            dma((2, 2, 6)),
            dma((2, 2, 6)),
            dma((2, 2, max(planes - 1, 1))),
            dma((2, 2, max(planes - 1, 1))),
            pltpu.SemaphoreType.REGULAR,
        ],
        compiler_params=pltpu.CompilerParams(
            collective_id=0, has_side_effects=True, vmem_limit_bytes=60 * 1024 * 1024
        ),
        name="window",
    )(owner_table, inputs, out_grad, ln_gain, layer_scale, w_in[0], w_out[0])
    factor = 1.0 / (tokens * dp_count)
    return pl.pallas_call(
        functools.partial(scale_kernel, factor),
        out_shape=(
            jax.ShapeDtypeStruct((1, block_a, width), F32),
            jax.ShapeDtypeStruct((1, block_g, hidden_width), F32),
        ),
        in_specs=[vmem, vmem],
        out_specs=(vmem, vmem),
        compiler_params=pltpu.CompilerParams(vmem_limit_bytes=60 * 1024 * 1024),
        name="mean",
    )(act, grad)


def solution(mesh):
    placed = (
        P(None, "dp", None),
        P("section", None),
        P("section", None, None),
        P("section", None, None),
        P("section", None),
        P(None, "dp", None),
        P(),
    )
    return jax.shard_map(
        functools.partial(body, mesh.shape["dp"], mesh.shape["section"]),
        mesh=mesh,
        in_specs=placed,
        out_specs=(P("section", "dp", None), P("section", "dp", None)),
        check_vma=False,
    )
```
